32 devices in a mesh: slab: 16 (over z, y, core), chan: 2 (over x).
Axes of the slice: x: 2, y: 2, z: 4, core: 2. Of those that a mesh axis runs over, the one named last changes fastest.
Arguments:
- activations: float32 [64, 64, 32, 128], P('chan', 'slab'), may hold values from -6 to 6
- kernel: float32 [64, 27, 64], P(None, None, 'chan'), may hold values from -0.15625 to 0.15625
- cotangent: float32 [64, 64, 32, 128], P('chan', 'slab'), may hold values from -6 to 6
Outputs:
- features: float32 [64, 64, 32, 128], P('chan', 'slab')
- input_grad: float32 [64, 64, 32, 128], P('chan', 'slab')
- weight_grad: float32 [64, 27, 64], P(None, None, 'chan')
The draws below stay inside these ranges and needn't reach their ends.
All inputs are finite; a program needn't handle non-finite values.
Results may differ from the reference program's by a relative error of at most 0.0003.
Values sent between devices are 32-bit elements; how exact they have to be, the bound alone decides.
No kernel may reach another device: no remote copies, remote signals or barrier semaphores. Data moves between devices by JAX's collectives and lax.ppermute only.
A program may use at most 192 MiB of HBM per device.

```python
import math
import jax
import jax.numpy as jnp
from jax import lax

CH = 64
HEIGHT = 32
WIDTH = 128
DEPTH = 64
CELLS = 262144


def block_scale(rng, dims, split, low, largest):
    level = 1.0
    for dim, shards_of in split:
        steps = jax.random.uniform(jax.random.fold_in(jax.random.fold_in(rng, 6), dim), (shards_of,), jnp.float32, low / len(split), largest / len(split))
        level = level * jnp.repeat(jnp.exp(steps), dims[dim] // shards_of).reshape((-1,) + (1,) * (len(dims) - 1 - dim))
    return level


def scatter_about(stream_key, dims, spread, bound, split=(), dtype=jnp.bfloat16):
    values = jax.random.normal(stream_key, dims, jnp.float32) * spread
    if len(split) > 0:
        values = block_scale(stream_key, dims, split, -0.22, 0.18) * values
    return jnp.clip(values, min=-bound, max=bound).astype(dtype)


def setup_inputs(seed: int = 0) -> dict:
    keys = jax.random.split(jax.random.key(seed), 4)
    activations = scatter_about(keys[0], (CH, DEPTH, HEIGHT, WIDTH), 1.0, 6.0, ((0, 2), (1, 16)), jnp.float32)
    kernel = scatter_about(keys[1], (CH, 27, CH), (27 * CH) ** -0.5, 0.15625, ((2, 2),), jnp.float32)
    cotangent = scatter_about(keys[2], (CH, DEPTH, HEIGHT, WIDTH), 1.0, 6.0, ((0, 2), (1, 16)), jnp.float32)
    return {"activations": activations, "kernel": kernel, "cotangent": cotangent}


def convolve(field, kernel):
    taps = kernel.reshape(CH, 3, 3, 3, CH).transpose(0, 4, 1, 2, 3)
    result = lax.conv_general_dilated(field[None], taps, (1, 1, 1), ((1, 1), (1, 1), (1, 1)), dimension_numbers=('NCDHW', 'OIDHW', 'NCDHW'), precision=lax.Precision.HIGHEST)
    return result[0]

def reference(activations, kernel, cotangent):
    features, pullback = jax.vjp(convolve, activations, kernel)
    input_grad, kernel_grad = pullback(cotangent)
    weight_grad = kernel_grad / math.sqrt(CELLS)
    return (features, input_grad, weight_grad)
```

```python
import functools
import math

import jax
import jax.numpy as jnp
from jax import lax
from jax.experimental import pallas as pl
from jax.experimental.pallas import tpu as pltpu
from jax.sharding import PartitionSpec as P

F32 = jnp.float32
BF16 = jnp.bfloat16


def split(x):
    hi = x.astype(BF16)
    return hi, (x - hi.astype(F32)).astype(BF16)


def fill_rows(dst_hi, dst_lo, plane, src, first, stride, chans, padded, height):
    blank = jnp.zeros((padded, dst_hi.shape[-1]), BF16)
    for dst in (dst_hi, dst_lo):
        dst[plane, pl.ds(0, padded), :] = blank
        dst[plane, pl.ds((height + 1) * padded, padded), :] = blank

    def one_row(row, carry):
        hi, lo = split(src[pl.ds(first + row, chans, stride=stride), :])
        start = pl.multiple_of((row + 1) * padded, padded)
        for dst, part in ((dst_hi, hi), (dst_lo, lo)):
            if padded != chans:
                fill = jnp.zeros((padded - chans, part.shape[1]), BF16)
                part = jnp.concatenate([part, fill], axis=0)
            dst[plane, pl.ds(start, padded), :] = part
        return carry

    lax.fori_loop(0, height, one_row, 0, unroll=4)


def fill_field(dst_hi, dst_lo, field, below, above, chans, padded, planes, height):
    fill_rows(dst_hi, dst_lo, 0, below, 0, height, chans, padded, height)
    fill_rows(dst_hi, dst_lo, planes + 1, above, 0, height, chans, padded, height)

    def one_plane(d, carry):
        fill_rows(
            dst_hi, dst_lo, d + 1, field, d * height, planes * height, chans, padded, height
        )
        return carry

    lax.fori_loop(0, planes, one_plane, 0)


def conv_kernel(dims, groups, has_acc, *refs):
    chans, padded, planes, height, outs = dims
    field, below, above, weight = refs[:4]
    refs = refs[4:]
    acc = None
    if has_acc:
        acc, refs = refs[0], refs[1:]
    results = refs[:groups]
    xh, xl = refs[groups:]
    d = pl.program_id(0)
    width = field.shape[-1]

    @pl.when(d == 0)
    def _():
        fill_field(xh, xl, field, below, above, chans, padded, planes, height)

    lane = lax.broadcasted_iota(jnp.int32, (groups * outs, width), 1)
    first = lane == 0
    last = lane == width - 1
    span = 3 * padded
    rows_out = groups * outs

    def one_pair(pair, carry):
        h = 2 * pair
        parts = []
        for src in (xh, xl):
            for i in range(3):
                block = src[d + i, pl.ds(pl.multiple_of(h * padded, padded), 4 * padded), :]
                parts.append(
                    jnp.concatenate([block[:span], block[padded : padded + span]], axis=1)
                )
        parts = parts + parts[:3]
        extra = weight.shape[1] - 9 * span
        if extra:
            parts.append(jnp.zeros((extra, 2 * width), BF16))
        y = jnp.dot(
            weight[...], jnp.concatenate(parts, axis=0), preferred_element_type=F32
        )
        for r in range(2):
            z = y[:, r * width : (r + 1) * width]
            left = pltpu.roll(z[:rows_out], 1, 1)
            right = pltpu.roll(z[2 * rows_out :], width - 1, 1)
            total = (
                z[rows_out : 2 * rows_out]
                + jnp.where(first, 0.0, left)
                + jnp.where(last, 0.0, right)
            )
            for g in range(groups):
                where = pl.ds(h + r, outs, stride=height)
                piece = total[g * outs : (g + 1) * outs]
                if acc is not None:
                    piece = piece + acc.reshape(outs * height, width)[where, :]
                results[g].reshape(outs * height, width)[where, :] = piece
        return carry

    lax.fori_loop(0, height // 2, one_pair, 0)


def conv(field, below, above, weight, outs, groups, acc=None):
    chans, planes, height, width = field.shape
    padded = -(-chans // 16) * 16
    flat = field.reshape(chans * planes * height, width)
    args = [flat, below.reshape(chans * height, width), above.reshape(chans * height, width), weight]
    whole = pl.BlockSpec(memory_space=pltpu.VMEM)
    plane_spec = pl.BlockSpec((outs, 1, height, width), lambda d: (0, d, 0, 0))
    in_specs = [whole] * 4
    if acc is not None:
        args.append(acc)
        in_specs.append(plane_spec)
    cells = planes * height * width
    shape = jax.ShapeDtypeStruct((outs, planes, height, width), F32)
    return pl.pallas_call(
        functools.partial(
            conv_kernel, (chans, padded, planes, height, outs), groups, acc is not None
        ),
        grid=(planes,),
        in_specs=in_specs,
        out_specs=[plane_spec] * groups,
        out_shape=[shape] * groups,
        scratch_shapes=[
            pltpu.VMEM((planes + 2, (height + 2) * padded, width), BF16) for _ in range(2)
        ],
        compiler_params=pltpu.CompilerParams(
            dimension_semantics=("arbitrary",), vmem_limit_bytes=32 << 20
        ),
        cost_estimate=pl.CostEstimate(
            flops=6 * 27 * chans * outs * groups * cells * 2,
            bytes_accessed=4 * (chans + outs * groups) * cells,
            transcendentals=0,
        ),
        name="conv",
    )(*args)


def grad_kernel(dims, field, below, above, cot, out, xh, xl, total):
    chans, padded, planes, height, rows = dims
    outs = cot.shape[0] // (planes * height)
    width = field.shape[-1]
    step = pl.program_id(0)
    span = 3 * padded

    @pl.when(step == 0)
    def _():
        fill_field(xh, xl, field, below, above, chans, padded, planes, height)
        total[...] = jnp.zeros_like(total)

    lane = lax.broadcasted_iota(jnp.int32, (outs, width), 1)
    first = lane == 0
    last = lane == width - 1
    group = padded_outs(outs)

    def one_block(block, carry):
        h = block * rows
        lhs = []
        for src in (xh, xl):
            for i in range(3):
                window = src[
                    step + i, pl.ds(pl.multiple_of(h * padded, padded), (rows + 2) * padded), :
                ]
                lhs.append(
                    jnp.concatenate(
                        [window[r * padded : r * padded + span] for r in range(rows)], axis=1
                    )
                )
        columns = []
        for r in range(rows):
            c = cot[pl.ds(step * height + h + r, outs, stride=planes * height), :]
            moved = [
                jnp.where(last, 0.0, pltpu.roll(c, width - 1, 1)),
                c,
                jnp.where(first, 0.0, pltpu.roll(c, 1, 1)),
            ]
            pieces = [split(m) for m in moved]
            high = [p[0] for p in pieces]
            low = [p[1] for p in pieces]
            gap = group - 3 * outs
            fill = [jnp.zeros((gap, width), BF16)] if gap else []
            columns.append(jnp.concatenate(high + fill + low + fill, axis=0))
        total[...] += lax.dot_general(
            jnp.concatenate(lhs, axis=0),
            jnp.concatenate(columns, axis=1),
            (((1,), (1,)), ((), ())),
            preferred_element_type=F32,
        )
        return carry

    lax.fori_loop(0, height // rows, one_block, 0)

    @pl.when(step == planes - 1)
    def _():
        half = 3 * span
        out[...] = (
            total[:half, :group] + total[:half, group:] + total[half:, :group]
        )


def padded_outs(outs):
    return -(-3 * outs // 128) * 128


def kernel_grad(field, below, above, cot):
    chans, planes, height, width = field.shape
    outs = cot.shape[0]
    padded = -(-chans // 16) * 16
    rows = 4
    group = padded_outs(outs)
    whole = pl.BlockSpec(memory_space=pltpu.VMEM)
    cells = planes * height * width
    return pl.pallas_call(
        functools.partial(grad_kernel, (chans, padded, planes, height, rows)),
        grid=(planes,),
        in_specs=[whole] * 4,
        out_specs=pl.BlockSpec((9 * padded, group), lambda d: (0, 0)),
        out_shape=jax.ShapeDtypeStruct((9 * padded, group), F32),
        scratch_shapes=[
            pltpu.VMEM((planes + 2, (height + 2) * padded, width), BF16) for _ in range(2)
        ]
        + [pltpu.VMEM((18 * padded, 2 * group), F32)],
        compiler_params=pltpu.CompilerParams(
            dimension_semantics=("arbitrary",), vmem_limit_bytes=32 << 20
        ),
        cost_estimate=pl.CostEstimate(
            flops=6 * 27 * chans * outs * cells * 2,
            bytes_accessed=4 * (chans + outs) * cells,
            transcendentals=0,
        ),
        name="kernel_grad",
    )(
        field.reshape(chans * planes * height, width),
        below.reshape(chans * height, width),
        above.reshape(chans * height, width),
        cot.reshape(outs * planes * height, width),
    )


def three_pass(matrix, padded):
    rows, taps, chans = matrix.shape
    matrix = jnp.pad(matrix, ((0, 0), (0, 0), (0, padded - chans)))
    matrix = matrix.reshape(rows, taps * padded)
    high = lax.reduce_precision(matrix, 8, 7)
    low = matrix - high
    wide = jnp.concatenate([high, high, low], axis=1)
    extra = -wide.shape[1] % 128
    return jnp.pad(wide, ((0, 0), (0, extra))).astype(BF16)


def slab_halo(field):
    count = lax.axis_size("slab")
    planes = field.shape[1]
    up = [(i, i + 1) for i in range(count - 1)]
    down = [(i + 1, i) for i in range(count - 1)]
    below = lax.ppermute(field[:, planes - 1 :], "slab", up)
    above = lax.ppermute(field[:, :1], "slab", down)
    return below, above


def slab_sum(value):
    count = lax.axis_size("slab")
    if count & (count - 1):
        return lax.psum(value, "slab")
    bit = 1
    while bit < count:
        value = value + lax.ppermute(value, "slab", [(i, i ^ bit) for i in range(count)])
        bit *= 2
    return value


def per_device(activations, kernel, cotangent):
    groups = lax.axis_size("chan")
    me = lax.axis_index("chan")
    channels, taps, cin = kernel.shape
    mine = channels // groups
    planes, height, width = activations.shape[1:]
    pad_in = -(-cin // 16) * 16
    pad_out = -(-mine // 16) * 16

    cots = [cotangent]
    for s in range(1, groups):
        cots.append(
            lax.ppermute(cotangent, "chan", [((i + s) % groups, i) for i in range(groups)])
        )
    act_halo = slab_halo(activations)
    cot_halo = slab_halo(cotangent)

    w = jnp.roll(kernel.reshape(groups, mine, 3, 3, 3, cin), -me, axis=0)
    forward = w.transpose(4, 0, 1, 2, 3, 5).reshape(3 * channels, 9, cin)
    forward = three_pass(forward, pad_in)
    flipped = w[:, :, ::-1, ::-1, ::-1].transpose(0, 4, 5, 2, 3, 1)
    backward = [three_pass(flipped[s].reshape(3 * cin, 9, mine), pad_out) for s in range(groups)]

    partial = conv(activations, *act_halo, forward, mine, groups)
    received = [
        lax.ppermute(partial[s], "chan", [(i, (i + s) % groups) for i in range(groups)])
        for s in range(1, groups)
    ]

    grads = [kernel_grad(activations, *act_halo, cotangent)]
    (input_grad,) = conv(cotangent, *cot_halo, backward[0], cin, 1)
    for s in range(1, groups):
        halo = slab_halo(cots[s])
        grads.append(kernel_grad(activations, *act_halo, cots[s]))
        (input_grad,) = conv(cots[s], *halo, backward[s], cin, 1, input_grad)

    summed = slab_sum(jnp.stack(grads))
    summed = summed.reshape(groups, 3, 3, pad_in, -1)[:, :, :, :cin, : 3 * mine]
    summed = summed.reshape(groups, 3, 3, cin, 3, mine)
    weight_grad = jnp.roll(summed.transpose(0, 5, 1, 2, 4, 3), me, axis=0)
    cells_all = planes * lax.axis_size("slab") * height * width
    weight_grad = weight_grad.reshape(channels, taps, cin) / math.sqrt(cells_all)

    features = partial[0]
    for part in received:
        features = features + part
    return features, input_grad, weight_grad


def solution(mesh):
    return jax.shard_map(
        per_device,
        mesh=mesh,
        in_specs=(
            P("chan", "slab", None, None),
            P(None, None, "chan"),
            P("chan", "slab", None, None),
        ),
        out_specs=(
            P("chan", "slab", None, None),
            P("chan", "slab", None, None),
            P(None, None, "chan"),
        ),
        check_vma=False,
    )
```

```python
import functools
import math

import jax
import jax.numpy as jnp
from jax import lax
from jax.experimental import pallas as pl
from jax.experimental.pallas import tpu as pltpu
from jax.sharding import PartitionSpec as P

F32 = jnp.float32
BF16 = jnp.bfloat16
ROWS = 8
WHOLE = pl.BlockSpec(memory_space=pltpu.VMEM)
SCALAR = pl.BlockSpec(memory_space=pltpu.SMEM)


def up_to(size, unit):
    return -(-size // unit) * unit


def split(x):
    hi = x.astype(BF16)
    return hi, (x - hi.astype(F32)).astype(BF16)


def params(steps=1):
    return pltpu.CompilerParams(
        dimension_semantics=("arbitrary",) * steps or None, vmem_limit_bytes=32 << 20
    )


def fill_plane(dst_hi, dst_lo, plane, load, chans, padded, height):
    width = dst_hi.shape[-1]
    blank = jnp.zeros((padded, width), BF16)
    for dst in (dst_hi, dst_lo):
        dst[plane, pl.ds(0, padded), :] = blank
        dst[plane, pl.ds((height + 1) * padded, padded), :] = blank

    def one_block(block, carry):
        rows = jnp.swapaxes(load(pl.ds(pl.multiple_of(ROWS * block, ROWS), ROWS)), 0, 1)
        if padded != chans:
            fill = jnp.zeros((ROWS, padded - chans, width), F32)
            rows = jnp.concatenate([rows, fill], axis=1)
        hi, lo = split(rows.reshape(ROWS * padded, width))
        start = pl.multiple_of((ROWS * block + 1) * padded, padded)
        dst_hi[plane, pl.ds(start, ROWS * padded), :] = hi
        dst_lo[plane, pl.ds(start, ROWS * padded), :] = lo
        return carry

    lax.fori_loop(0, height // ROWS, one_block, 0, unroll=True)


def fill_field(dst_hi, dst_lo, field, below, above, chans, padded, planes, height):
    fill_plane(dst_hi, dst_lo, 0, lambda s: below[:, 0, s, :], chans, padded, height)
    fill_plane(dst_hi, dst_lo, planes + 1, lambda s: above[:, 0, s, :], chans, padded, height)

    def one_plane(d, carry):
        fill_plane(dst_hi, dst_lo, d + 1, lambda s: field[:, d, s, :], chans, padded, height)
        return carry

    lax.fori_loop(0, planes, one_plane, 0)


def conv_kernel(dims, sizes, unroll, has_acc, *refs):
    chans, padded, planes, height = dims
    field, below, above, weight = refs[:4]
    refs = refs[4:]
    acc = None
    if has_acc:
        acc, refs = refs[0], refs[1:]
    results = refs[: len(sizes)]
    xh, xl = refs[len(sizes) :]
    d = pl.program_id(0)
    width = field.shape[-1]
    rows_out = sum(sizes)
    span = 3 * padded

    @pl.when(d == 0)
    def _():
        fill_field(xh, xl, field, below, above, chans, padded, planes, height)

    lane = lax.broadcasted_iota(jnp.int32, (rows_out, width), 1)
    first = lane == 0
    last = lane == width - 1

    def one_block(block, carry):
        h = ROWS * block
        parts = []
        for src in (xh, xl):
            for i in range(3):
                window = src[
                    d + i, pl.ds(pl.multiple_of(h * padded, padded), (ROWS + 2) * padded), :
                ]
                parts.append(
                    jnp.concatenate(
                        [window[r * padded : r * padded + span] for r in range(ROWS)], axis=1
                    )
                )
        parts = parts + parts[:3]
        extra = weight.shape[1] - 9 * span
        if extra:
            parts.append(jnp.zeros((extra, ROWS * width), BF16))
        y = jnp.dot(
            weight[...], jnp.concatenate(parts, axis=0), preferred_element_type=F32
        )
        rows = []
        for r in range(ROWS):
            z = y[:, r * width : (r + 1) * width]
            left = jnp.where(first, 0.0, pltpu.roll(z[:rows_out], 1, 1))
            right = jnp.where(last, 0.0, pltpu.roll(z[2 * rows_out :], width - 1, 1))
            rows.append(z[rows_out : 2 * rows_out] + left + right)
        swapped = jnp.swapaxes(jnp.stack(rows), 0, 1)
        where = pl.ds(pl.multiple_of(h, ROWS), ROWS)
        start = 0
        for ref, size in zip(results, sizes):
            piece = swapped[start : start + size]
            if acc is not None:
                piece = piece + acc[:, 0, where, :]
            ref[:, 0, where, :] = piece
            start += size
        return carry

    lax.fori_loop(0, height // ROWS, one_block, 0, unroll=unroll)


def conv(field, below, above, weight, sizes, unroll, acc=None):
    chans, planes, height, width = field.shape
    padded = up_to(chans, 16)

    def plane_spec(size):
        return pl.BlockSpec((size, 1, height, width), lambda d: (0, d, 0, 0))

    args = [field, below, above, weight]
    in_specs = [WHOLE] * 4
    if acc is not None:
        args.append(acc)
        in_specs.append(plane_spec(sizes[0]))
    cells = planes * height * width
    return pl.pallas_call(
        functools.partial(
            conv_kernel, (chans, padded, planes, height), sizes, unroll, acc is not None
        ),
        grid=(planes,),
        in_specs=in_specs,
        out_specs=[plane_spec(size) for size in sizes],
        out_shape=[jax.ShapeDtypeStruct((size, planes, height, width), F32) for size in sizes],
        scratch_shapes=[
            pltpu.VMEM((planes + 2, (height + 2) * padded, width), BF16) for _ in range(2)
        ],
        compiler_params=params(),
        cost_estimate=pl.CostEstimate(
            flops=6 * 27 * chans * sum(sizes) * cells * 2 // 20,
            bytes_accessed=4 * (chans + sum(sizes)) * cells // 20,
            transcendentals=0,
        ),
        name="conv",
    )(*args)


def grad_kernel(dims, others, *refs):
    chans, padded, planes, height = dims
    field, below, above, cot = refs[:4]
    done = refs[4 : 4 + others]
    out, xh, xl, total = refs[4 + others :]
    outs = cot.shape[0]
    width = field.shape[-1]
    step = pl.program_id(0)
    span = 3 * padded
    half = 3 * span
    group = up_to(3 * outs, 128)

    @pl.when(step == 0)
    def _():
        fill_field(xh, xl, field, below, above, chans, padded, planes, height)
        total[...] = jnp.zeros_like(total)

    lane = lax.broadcasted_iota(jnp.int32, (outs, width), 1)
    first = lane == 0
    last = lane == width - 1
    lhs = []
    for src in (xh, xl):
        for i in range(3):
            window = src[step + i]
            lhs.append(
                jnp.concatenate(
                    [window[r * padded : r * padded + span] for r in range(height)], axis=1
                )
            )
    columns = []
    for block in range(height // ROWS):
        rows = jnp.swapaxes(cot[:, 0, pl.ds(ROWS * block, ROWS), :], 0, 1)
        for r in range(ROWS):
            c = rows[r]
            moved = [
                jnp.where(last, 0.0, pltpu.roll(c, width - 1, 1)),
                c,
                jnp.where(first, 0.0, pltpu.roll(c, 1, 1)),
            ]
            pieces = [split(m) for m in moved]
            gap = group - 3 * outs
            fill = [jnp.zeros((gap, width), BF16)] if gap else []
            columns.append(
                jnp.concatenate(
                    [p[0] for p in pieces] + fill + [p[1] for p in pieces] + fill, axis=0
                )
            )
    total[...] += lax.dot_general(
        jnp.concatenate(lhs, axis=0),
        jnp.concatenate(columns, axis=1),
        (((1,), (1,)), ((), ())),
        preferred_element_type=F32,
    )

    @pl.when(step == planes - 1)
    def _():
        for index, ref in enumerate(done):
            out[index] = ref[0]
        out[others] = total[:half, :group] + total[:half, group:] + total[half:, :group]


def kernel_grad(field, below, above, cot, done=()):
    chans, planes, height, width = field.shape
    outs = cot.shape[0]
    padded = up_to(chans, 16)
    group = up_to(3 * outs, 128)
    cells = planes * height * width
    count = len(done) + 1
    return pl.pallas_call(
        functools.partial(grad_kernel, (chans, padded, planes, height), len(done)),
        grid=(planes,),
        in_specs=[WHOLE] * 3
        + [pl.BlockSpec((outs, 1, height, width), lambda d: (0, d, 0, 0))]
        + [WHOLE] * len(done),
        out_specs=pl.BlockSpec((count, 9 * padded, group), lambda d: (0, 0, 0)),
        out_shape=jax.ShapeDtypeStruct((count, 9 * padded, group), F32),
        scratch_shapes=[
            pltpu.VMEM((planes + 2, (height + 2) * padded, width), BF16) for _ in range(2)
        ]
        + [pltpu.VMEM((18 * padded, 2 * group), F32)],
        compiler_params=params(),
        cost_estimate=pl.CostEstimate(
            flops=6 * 27 * chans * outs * cells * 2 // 20,
            bytes_accessed=4 * (chans + outs) * cells // 20,
            transcendentals=0,
        ),
        name="kernel_grad",
    )(field, below, above, cot, *done)


def three_parts(matrix, wide):
    hi, lo = split(matrix)
    parts = [hi, hi, lo]
    extra = wide - 3 * matrix.shape[1]
    if extra:
        parts.append(jnp.zeros((matrix.shape[0], extra), BF16))
    return jnp.concatenate(parts, axis=1)


def weight_kernel(groups, me, taps, forward, *refs):
    backward, turned = refs[:groups], refs[groups]
    cin, channels = taps.shape[1:]
    mine = channels // groups
    pad_in = up_to(cin, 16)
    pad_out = up_to(mine, 16)
    for k in range(3):
        blocks = []
        for tap in range(9):
            blocks.append(taps[3 * tap + k])
            if pad_in != cin:
                blocks.append(jnp.zeros((pad_in - cin, channels), F32))
        turned[...] = jnp.concatenate(blocks, axis=0).T
        for g in range(groups):
            owner = lax.rem(me[0] + g, groups)
            rows = turned[pl.ds(pl.multiple_of(owner * mine, mine), mine), :]
            forward[pl.ds(k * channels + g * mine, mine), :] = three_parts(
                rows, forward.shape[1]
            )
    for s in range(groups):
        owner = lax.rem(me[0] + s, groups)
        for k in range(3):
            blocks = []
            for tap in range(9):
                block = taps[26 - 3 * tap - k]
                chosen = block[:, :mine]
                for q in range(1, groups):
                    chosen = jnp.where(owner == q, block[:, q * mine : (q + 1) * mine], chosen)
                blocks.append(chosen)
                if pad_out != mine:
                    blocks.append(jnp.zeros((cin, pad_out - mine), F32))
            backward[s][pl.ds(k * cin, cin), :] = three_parts(
                jnp.concatenate(blocks, axis=1), backward[s].shape[1]
            )


def weight_matrices(me, taps, groups):
    _, cin, channels = taps.shape
    mine = channels // groups
    pad_in = up_to(cin, 16)
    wide_in = up_to(27 * pad_in, 128)
    wide_out = up_to(27 * up_to(mine, 16), 128)
    return pl.pallas_call(
        functools.partial(weight_kernel, groups),
        in_specs=[SCALAR, WHOLE],
        out_specs=[WHOLE] * (groups + 1),
        out_shape=[jax.ShapeDtypeStruct((3 * channels, wide_in), BF16)]
        + [jax.ShapeDtypeStruct((3 * cin, wide_out), BF16)] * groups,
        scratch_shapes=[pltpu.VMEM((channels, 9 * pad_in), F32)],
        compiler_params=params(0),
        name="weights",
    )(me, taps)


def finish_kernel(groups, scale, me, mine_ref, other_ref, out):
    cin, channels = out.shape[1:]
    mine = channels // groups
    padded = mine_ref.shape[1] // 9
    totals = [(mine_ref[s] + other_ref[s]) * scale for s in range(groups)]
    for k in range(3):
        pieces = [t[:, k * mine : (k + 1) * mine] for t in totals]
        blocks = []
        for q in range(groups):
            source = lax.rem(q - me[0] + groups, groups)
            chosen = pieces[0]
            for s in range(1, groups):
                chosen = jnp.where(source == s, pieces[s], chosen)
            blocks.append(chosen)
        wide = jnp.concatenate(blocks, axis=1)
        for tap in range(9):
            out[3 * tap + k] = wide[tap * padded : tap * padded + cin]


def finish(me, value, other, groups, cin, channels, scale):
    return pl.pallas_call(
        functools.partial(finish_kernel, groups, scale),
        in_specs=[SCALAR, WHOLE, WHOLE],
        out_specs=WHOLE,
        out_shape=jax.ShapeDtypeStruct((27, cin, channels), F32),
        compiler_params=params(0),
        name="finish",
    )(me, value, other)


def add_kernel(base, piece, out):
    out[...] = base[...] + piece[...]


def add_into(base, piece, first, block):
    shape = (block,) + base.shape[1:]
    spec = pl.BlockSpec(shape, lambda c: (first // block + c, 0, 0, 0))
    return pl.pallas_call(
        add_kernel,
        grid=(piece.shape[0] // block,),
        in_specs=[spec, pl.BlockSpec(shape, lambda c: (c, 0, 0, 0))],
        out_specs=spec,
        out_shape=jax.ShapeDtypeStruct(base.shape, F32),
        input_output_aliases={0: 0},
        compiler_params=params(),
        cost_estimate=pl.CostEstimate(
            flops=piece.size, bytes_accessed=12 * piece.size, transcendentals=0
        ),
        name="add_into",
    )(base, piece)


def slab_halo(field):
    count = lax.axis_size("slab")
    planes = field.shape[1]
    up = [(i, i + 1) for i in range(count - 1)]
    down = [(i + 1, i) for i in range(count - 1)]
    top, bottom = field[:, planes - 1 :], field[:, :1]
    field, top, bottom = lax.optimization_barrier((field, top, bottom))
    return field, (lax.ppermute(top, "slab", up), lax.ppermute(bottom, "slab", down))


def slab_sum(value):
    count = lax.axis_size("slab")
    if count & (count - 1):
        value = lax.psum(value, "slab")
        return value, jnp.zeros_like(value)
    bit = 1
    other = jnp.zeros_like(value) if count == 1 else None
    while bit < count:
        if other is not None:
            value = value + other
        other = lax.ppermute(value, "slab", [(i, i ^ bit) for i in range(count)])
        bit *= 2
    return value, other


def per_device(activations, kernel, cotangent):
    groups = lax.axis_size("chan")
    me = lax.axis_index("chan").reshape(1)
    channels, taps, cin = kernel.shape
    mine = channels // groups
    planes, height, width = activations.shape[1:]
    tail = max(mine // 4, 1)
    pieces = (mine - tail, tail)

    cots = [cotangent]
    for s in range(1, groups):
        cots.append(
            lax.ppermute(cotangent, "chan", [((i + s) % groups, i) for i in range(groups)])
        )
    activations, act_halo = slab_halo(activations)
    forward, *backward = weight_matrices(me, kernel.transpose(1, 2, 0), groups)

    features, *partial = conv(
        activations, *act_halo, forward, (mine,) + pieces * (groups - 1), 2
    )
    received = []
    for s in range(1, groups):
        for part in partial[2 * (s - 1) : 2 * s]:
            received.append(
                lax.ppermute(part, "chan", [(i, (i + s) % groups) for i in range(groups)])
            )

    own, _ = lax.optimization_barrier((cotangent, partial[0]))
    own, cot_halo = slab_halo(own)
    grads = [kernel_grad(activations, *act_halo, own)]
    (input_grad,) = conv(own, *cot_halo, backward[0], (cin,), 4)
    for s in range(1, groups):
        cots[s], input_grad = lax.optimization_barrier((cots[s], input_grad))
        cots[s], halo = slab_halo(cots[s])
        done = grads if s == groups - 1 else ()
        grads.append(kernel_grad(activations, *act_halo, cots[s], done))
        (input_grad,) = conv(cots[s], *halo, backward[s], (cin,), 4, input_grad)

    cells_all = planes * lax.axis_size("slab") * height * width
    value, other = slab_sum(grads[-1])
    weight_grad = finish(me, value, other, groups, cin, channels, 1.0 / math.sqrt(cells_all))

    *received, input_grad = lax.optimization_barrier((*received, input_grad))
    for index, part in enumerate(received):
        first = 0 if index % 2 == 0 else pieces[0]
        features = add_into(features, part, first, tail)
    return features, input_grad, weight_grad.transpose(2, 0, 1)


def solution(mesh):
    return jax.shard_map(
        per_device,
        mesh=mesh,
        in_specs=(
            P("chan", "slab", None, None),
            P(None, None, "chan"),
            P("chan", "slab", None, None),
        ),
        out_specs=(
            P("chan", "slab", None, None),
            P("chan", "slab", None, None),
            P(None, None, "chan"),
        ),
        check_vma=False,
    )
```

```python
import functools
import math

import jax
import jax.numpy as jnp
from jax import lax
from jax.experimental import pallas as pl
from jax.experimental.pallas import tpu as pltpu
from jax.sharding import PartitionSpec as P

F32 = jnp.float32
BF16 = jnp.bfloat16
ROWS = 8
VMEM_LIMIT = 16 << 20
WHOLE = pl.BlockSpec(memory_space=pltpu.VMEM)
SCALAR = pl.BlockSpec(memory_space=pltpu.SMEM)


def up_to(size, unit):
    return -(-size // unit) * unit


def split(x):
    hi = x.astype(BF16)
    return hi, (x - hi.astype(F32)).astype(BF16)


def params(steps=1):
    return pltpu.CompilerParams(
        dimension_semantics=("arbitrary",) * steps or None, vmem_limit_bytes=VMEM_LIMIT
    )


def fill_plane(dst_hi, dst_lo, plane, load, chans, padded, height):
    width = dst_hi.shape[-1]
    blank = jnp.zeros((padded, width), BF16)
    for dst in (dst_hi, dst_lo):
        dst[plane, pl.ds(0, padded), :] = blank
        dst[plane, pl.ds((height + 1) * padded, padded), :] = blank

    def one_block(block, carry):
        rows = jnp.swapaxes(load(pl.ds(pl.multiple_of(ROWS * block, ROWS), ROWS)), 0, 1)
        if padded != chans:
            fill = jnp.zeros((ROWS, padded - chans, width), F32)
            rows = jnp.concatenate([rows, fill], axis=1)
        hi, lo = split(rows.reshape(ROWS * padded, width))
        start = pl.multiple_of((ROWS * block + 1) * padded, padded)
        dst_hi[plane, pl.ds(start, ROWS * padded), :] = hi
        dst_lo[plane, pl.ds(start, ROWS * padded), :] = lo
        return carry

    lax.fori_loop(0, height // ROWS, one_block, 0, unroll=True)


def conv_kernel(dims, sizes, unroll, has_acc, *refs):
    chans, padded, planes, height = dims
    field, sibling, neighbour, weight, bit = refs[:5]
    refs = refs[5:]
    acc = None
    if has_acc:
        acc, refs = refs[0], refs[1:]
    results = refs[: len(sizes)]
    xh, xl = refs[len(sizes) :]
    step = pl.program_id(0)
    d = step - 1
    width = field.shape[-1]
    rows_out = sum(sizes)
    span = 3 * padded

    @pl.when(step == 0)
    def _():
        for ref, side in ((sibling, 1 - bit[0]), (neighbour, bit[0])):
            fill_plane(
                xh, xl, side * (planes + 1), lambda s, r=ref: r[:, 0, s, :], chans, padded, height
            )

    @pl.when(step < planes)
    def _():
        fill_plane(xh, xl, step + 1, lambda s: field[:, 0, s, :], chans, padded, height)

    lane = lax.broadcasted_iota(jnp.int32, (rows_out, width), 1)
    first = lane == 0
    last = lane == width - 1

    def one_block(block, carry):
        h = ROWS * block
        parts = []
        for src in (xh, xl):
            for i in range(3):
                window = src[
                    d + i, pl.ds(pl.multiple_of(h * padded, padded), (ROWS + 2) * padded), :
                ]
                parts.append(
                    jnp.concatenate(
                        [window[r * padded : r * padded + span] for r in range(ROWS)], axis=1
                    )
                )
        parts = parts + parts[:3]
        extra = weight.shape[1] - 9 * span
        if extra:
            parts.append(jnp.zeros((extra, ROWS * width), BF16))
        y = jnp.dot(
            weight[...], jnp.concatenate(parts, axis=0), preferred_element_type=F32
        )
        rows = []
        for r in range(ROWS):
            z = y[:, r * width : (r + 1) * width]
            left = jnp.where(first, 0.0, pltpu.roll(z[:rows_out], 1, 1))
            right = jnp.where(last, 0.0, pltpu.roll(z[2 * rows_out :], width - 1, 1))
            rows.append(z[rows_out : 2 * rows_out] + left + right)
        swapped = jnp.swapaxes(jnp.stack(rows), 0, 1)
        where = pl.ds(pl.multiple_of(h, ROWS), ROWS)
        start = 0
        for ref, size in zip(results, sizes):
            piece = swapped[start : start + size]
            if acc is not None:
                piece = piece + acc[:, 0, where, :]
            ref[:, 0, where, :] = piece
            start += size
        return carry

    @pl.when(step > 0)
    def _():
        lax.fori_loop(0, height // ROWS, one_block, 0, unroll=unroll)


def conv(field, halo, weight, bit, sizes, unroll, acc=None, keep=False):
    chans, planes, height, width = field.shape
    padded = up_to(chans, 16)

    def plane_spec(size):
        return pl.BlockSpec(
            (size, 1, height, width), lambda d: (0, jnp.maximum(d - 1, 0), 0, 0)
        )

    args = [field, *halo, weight, bit]
    in_specs = [
        pl.BlockSpec(
            (chans, 1, height, width), lambda d: (0, jnp.minimum(d, planes - 1), 0, 0)
        )
    ]
    in_specs += [WHOLE] * 3 + [SCALAR]
    if acc is not None:
        args.append(acc)
        in_specs.append(plane_spec(sizes[0]))
    cells = planes * height * width
    held = (planes + 2, (height + 2) * padded, width)
    count = 2 if keep else 0
    return pl.pallas_call(
        functools.partial(
            conv_kernel, (chans, padded, planes, height), sizes, unroll, acc is not None
        ),
        grid=(planes + 1,),
        in_specs=in_specs,
        out_specs=[plane_spec(size) for size in sizes] + [WHOLE] * count,
        out_shape=[jax.ShapeDtypeStruct((size, planes, height, width), F32) for size in sizes]
        + [jax.ShapeDtypeStruct(held, BF16)] * count,
        scratch_shapes=[pltpu.VMEM(held, BF16)] * (2 - count),
        compiler_params=params(),
        cost_estimate=pl.CostEstimate(
            flops=6 * 27 * chans * sum(sizes) * cells * 2 // 20,
            bytes_accessed=4 * (chans + sum(sizes)) * cells // 20,
            transcendentals=0,
        ),
        name="conv",
    )(*args)


def grad_kernel(dims, others, *refs):
    padded, planes, height, width = dims
    xh, xl, cot, bit = refs[:4]
    done = refs[4 : 4 + others]
    *outs_refs, total = refs[4 + others :]
    outs = cot.shape[0]
    step = pl.program_id(0)
    span = 3 * padded
    half = 3 * span
    group = up_to(3 * outs, 128)

    @pl.when(step == 0)
    def _():
        total[...] = jnp.zeros_like(total)

    lane = lax.broadcasted_iota(jnp.int32, (outs, width), 1)
    first = lane == 0
    last = lane == width - 1
    lhs = []
    for src in (xh, xl):
        for i in range(3):
            window = src[step + i]
            lhs.append(
                jnp.concatenate(
                    [window[r * padded : r * padded + span] for r in range(height)], axis=1
                )
            )
    columns = []
    for block in range(height // ROWS):
        rows = jnp.swapaxes(cot[:, 0, pl.ds(ROWS * block, ROWS), :], 0, 1)
        for r in range(ROWS):
            c = rows[r]
            moved = [
                jnp.where(last, 0.0, pltpu.roll(c, width - 1, 1)),
                c,
                jnp.where(first, 0.0, pltpu.roll(c, 1, 1)),
            ]
            pieces = [split(m) for m in moved]
            gap = group - 3 * outs
            fill = [jnp.zeros((gap, width), BF16)] if gap else []
            columns.append(
                jnp.concatenate(
                    [p[0] for p in pieces] + fill + [p[1] for p in pieces] + fill, axis=0
                )
            )
    total[...] += lax.dot_general(
        jnp.concatenate(lhs, axis=0),
        jnp.concatenate(columns, axis=1),
        (((1,), (1,)), ((), ())),
        preferred_element_type=F32,
    )

    @pl.when(step == planes - 1)
    def _():
        summed = total[:half, :group] + total[:half, group:] + total[half:, :group]
        if len(outs_refs) == 1:
            outs_refs[0][...] = summed
        else:
            total[:half, :group] = summed
            rows = half // 2
            kept = pl.multiple_of(bit[0] * rows, 8)
            sent = pl.multiple_of((1 - bit[0]) * rows, 8)
            for ref, start in zip(outs_refs, (kept, sent)):
                for index, other in enumerate(done):
                    ref[index] = other[pl.ds(start, rows), :]
                ref[others] = total[pl.ds(start, rows), :group]


def kernel_grad(xh, xl, cot, bit, done=None):
    outs, planes, height, width = cot.shape
    padded = xh.shape[1] // (height + 2)
    group = up_to(3 * outs, 128)
    cells = planes * height * width
    rows = 9 * padded
    earlier = () if done is None else tuple(done)
    shape = (rows, group) if done is None else (len(earlier) + 1, rows // 2, group)
    shapes = [jax.ShapeDtypeStruct(shape, F32)] * (1 if done is None else 2)
    return pl.pallas_call(
        functools.partial(grad_kernel, (padded, planes, height, width), len(earlier)),
        grid=(planes,),
        in_specs=[WHOLE] * 2
        + [pl.BlockSpec((outs, 1, height, width), lambda d: (0, d, 0, 0)), SCALAR]
        + [WHOLE] * len(earlier),
        out_specs=[WHOLE] * len(shapes),
        out_shape=shapes,
        scratch_shapes=[pltpu.VMEM((2 * rows, 2 * group), F32)],
        compiler_params=params(),
        cost_estimate=pl.CostEstimate(
            flops=6 * 3 * rows * outs * cells * 2 // 20,
            bytes_accessed=8 * outs * cells // 20,
            transcendentals=0,
        ),
        name="kernel_grad",
    )(xh, xl, cot, bit, *earlier)


def three_parts(matrix, wide):
    hi, lo = split(matrix)
    parts = [hi, hi, lo]
    extra = wide - 3 * matrix.shape[1]
    if extra:
        parts.append(jnp.zeros((matrix.shape[0], extra), BF16))
    return jnp.concatenate(parts, axis=1)


def weight_kernel(groups, me, taps, forward, *refs):
    backward, turned = refs[:groups], refs[groups]
    cin, channels = taps.shape[1:]
    mine = channels // groups
    pad_in = up_to(cin, 16)
    pad_out = up_to(mine, 16)
    for k in range(3):
        blocks = []
        for tap in range(9):
            blocks.append(taps[3 * tap + k])
            if pad_in != cin:
                blocks.append(jnp.zeros((pad_in - cin, channels), F32))
        turned[...] = jnp.concatenate(blocks, axis=0).T
        for g in range(groups):
            owner = lax.rem(me[0] + g, groups)
            rows = turned[pl.ds(pl.multiple_of(owner * mine, mine), mine), :]
            forward[pl.ds(k * channels + g * mine, mine), :] = three_parts(
                rows, forward.shape[1]
            )
    for s in range(groups):
        owner = lax.rem(me[0] + s, groups)
        for k in range(3):
            blocks = []
            for tap in range(9):
                block = taps[26 - 3 * tap - k]
                chosen = block[:, :mine]
                for q in range(1, groups):
                    chosen = jnp.where(owner == q, block[:, q * mine : (q + 1) * mine], chosen)
                blocks.append(chosen)
                if pad_out != mine:
                    blocks.append(jnp.zeros((cin, pad_out - mine), F32))
            backward[s][pl.ds(k * cin, cin), :] = three_parts(
                jnp.concatenate(blocks, axis=1), backward[s].shape[1]
            )


def weight_matrices(me, taps, groups):
    _, cin, channels = taps.shape
    mine = channels // groups
    pad_in = up_to(cin, 16)
    wide_in = up_to(27 * pad_in, 128)
    wide_out = up_to(27 * up_to(mine, 16), 128)
    return pl.pallas_call(
        functools.partial(weight_kernel, groups),
        in_specs=[SCALAR, WHOLE],
        out_specs=[WHOLE] * (groups + 1),
        out_shape=[jax.ShapeDtypeStruct((3 * channels, wide_in), BF16)]
        + [jax.ShapeDtypeStruct((3 * cin, wide_out), BF16)] * groups,
        scratch_shapes=[pltpu.VMEM((channels, 9 * pad_in), F32)],
        compiler_params=params(0),
        name="weights",
    )(me, taps)


def finish_kernel(groups, scale, me, bit, mine_ref, other_ref, out):
    cin, channels = out.shape[1:]
    mine = channels // groups
    padded = 2 * mine_ref.shape[1] // 9
    low = bit[0] == 0
    totals = []
    for s in range(groups):
        a, b = mine_ref[s] * scale, other_ref[s] * scale
        totals.append(jnp.concatenate([jnp.where(low, a, b), jnp.where(low, b, a)], axis=0))
    for k in range(3):
        pieces = [t[:, k * mine : (k + 1) * mine] for t in totals]
        blocks = []
        for q in range(groups):
            source = lax.rem(q - me[0] + groups, groups)
            chosen = pieces[0]
            for s in range(1, groups):
                chosen = jnp.where(source == s, pieces[s], chosen)
            blocks.append(chosen)
        wide = jnp.concatenate(blocks, axis=1)
        for tap in range(9):
            out[3 * tap + k] = wide[tap * padded : tap * padded + cin]


def finish(me, bit, value, other, groups, cin, channels, scale):
    return pl.pallas_call(
        functools.partial(finish_kernel, groups, scale),
        in_specs=[SCALAR, SCALAR, WHOLE, WHOLE],
        out_specs=WHOLE,
        out_shape=jax.ShapeDtypeStruct((27, cin, channels), F32),
        compiler_params=params(0),
        name="finish",
    )(me, bit, value, other)


def add_kernel(base, piece, out):
    out[...] = base[...] + piece[...]


def add_into(base, piece, first, block):
    shape = (block,) + base.shape[1:]
    spec = pl.BlockSpec(shape, lambda c: (first // block + c, 0, 0, 0))
    return pl.pallas_call(
        add_kernel,
        grid=(piece.shape[0] // block,),
        in_specs=[spec, pl.BlockSpec(shape, lambda c: (c, 0, 0, 0))],
        out_specs=spec,
        out_shape=jax.ShapeDtypeStruct(base.shape, F32),
        input_output_aliases={0: 0},
        compiler_params=params(),
        cost_estimate=pl.CostEstimate(
            flops=piece.size, bytes_accessed=12 * piece.size, transcendentals=0
        ),
        name="add_into",
    )(base, piece)


def cut_edges(field, bit):
    ends = field.shape[1] - 1
    to_sibling = lax.dynamic_slice_in_dim(field, (1 - bit[0]) * ends, 1, axis=1)
    to_neighbour = lax.dynamic_slice_in_dim(field, bit[0] * ends, 1, axis=1)
    return lax.optimization_barrier((field, to_sibling, to_neighbour))


def slab_halo(to_sibling, to_neighbour):
    count = lax.axis_size("slab")
    across = [(i, i + 1) for i in range(1, count - 1, 2)]
    across += [(j, i) for i, j in across]
    return slab_swap(to_sibling, 1), lax.ppermute(to_neighbour, "slab", across)


def slab_swap(value, bit):
    return lax.ppermute(
        value, "slab", [(i, i ^ bit) for i in range(lax.axis_size("slab"))]
    )


def per_device(activations, kernel, cotangent):
    groups = lax.axis_size("chan")
    slabs = lax.axis_size("slab")
    assert slabs >= 4 and slabs & (slabs - 1) == 0 and groups > 1
    me = lax.axis_index("chan").reshape(1)
    bit = lax.rem(lax.axis_index("slab"), 2).reshape(1)
    channels, taps, cin = kernel.shape
    mine = channels // groups
    planes, height, width = activations.shape[1:]
    tail = max(mine // 4, 1)
    pieces = (mine - tail, tail)
    after = lax.optimization_barrier

    cots = [cotangent]
    for s in range(1, groups):
        cots.append(
            lax.ppermute(cotangent, "chan", [((i + s) % groups, i) for i in range(groups)])
        )
    activations, *edges = cut_edges(activations, bit)
    own, *edges = after((cotangent, *edges))
    act_halo = slab_halo(*edges)
    own, *edges = cut_edges(own, bit)
    cot_halo = slab_halo(*edges)
    forward, *backward = weight_matrices(me, kernel.transpose(1, 2, 0), groups)

    features, *partial, xh, xl = conv(
        activations, act_halo, forward, bit, (mine,) + pieces * (groups - 1), 2, keep=True
    )
    received = []
    for s in range(1, groups):
        for part in partial[2 * (s - 1) : 2 * s]:
            received.append(
                lax.ppermute(part, "chan", [(i, (i + s) % groups) for i in range(groups)])
            )

    grads = list(kernel_grad(xh, xl, own, bit))
    (input_grad,) = conv(own, cot_halo, backward[0], bit, (cin,), 4)
    for s in range(1, groups):
        cot, input_grad, *grads = after((cots[s], input_grad, *grads))
        cot, *edges = cut_edges(cot, bit)
        halo = slab_halo(*edges)
        if s < groups - 1:
            grads += kernel_grad(xh, xl, cot, bit)
        else:
            kept, sent = kernel_grad(xh, xl, cot, bit, grads)
            kept, sent, *halo = after((kept, sent, *halo))
            value = kept + slab_swap(sent, 1)
            value, cot = after((value, cot))
            other = slab_swap(value, 2)
        (input_grad,) = conv(cot, halo, backward[s], bit, (cin,), 4, input_grad)

    other, input_grad = after((other, input_grad))
    value = value + other
    step = 4
    while step < slabs // 2:
        value = value + slab_swap(value, step)
        step *= 2
    first_parts, last_part = received[:-1], received[-1]
    *first_parts, value = after((*first_parts, value))
    other = slab_swap(value, step)
    for index, part in enumerate(first_parts):
        features = add_into(features, part, 0 if index % 2 == 0 else pieces[0], tail)
    other, features = after((other, features))
    value = value + other
    cells_all = planes * slabs * height * width
    weight_grad = finish(
        me, bit, value, slab_swap(value, 1), groups, cin, channels, 1.0 / math.sqrt(cells_all)
    )
    weight_grad, features, last_part = after((weight_grad, features, last_part))
    features = add_into(features, last_part, pieces[0], tail)
    return features, input_grad, weight_grad.transpose(2, 0, 1)


def solution(mesh):
    return jax.shard_map(
        per_device,
        mesh=mesh,
        in_specs=(
            P("chan", "slab", None, None),
            P(None, None, "chan"),
            P("chan", "slab", None, None),
        ),
        out_specs=(
            P("chan", "slab", None, None),
            P("chan", "slab", None, None),
            P(None, None, "chan"),
        ),
        check_vma=False,
    )
```

```python
import functools
import math

import jax
import jax.numpy as jnp
from jax import lax
from jax.experimental import pallas as pl
from jax.experimental.pallas import tpu as pltpu
from jax.sharding import PartitionSpec as P

F32 = jnp.float32
BF16 = jnp.bfloat16
ROWS = 8
VMEM_LIMIT = 16 << 20
COST_SHARE = 20
WHOLE = pl.BlockSpec(memory_space=pltpu.VMEM)
SCALAR = pl.BlockSpec(memory_space=pltpu.SMEM)


def up_to(size, unit):
    return -(-size // unit) * unit


def split(x):
    hi = x.astype(BF16)
    return hi, (x - hi.astype(F32)).astype(BF16)


def params(steps=1):
    return pltpu.CompilerParams(
        dimension_semantics=("arbitrary",) * steps or None, vmem_limit_bytes=VMEM_LIMIT
    )


def fill_plane(dst_hi, dst_lo, plane, load, chans, padded, height):
    width = dst_hi.shape[-1]
    blank = jnp.zeros((padded, width), BF16)
    for dst in (dst_hi, dst_lo):
        dst[plane, pl.ds(0, padded), :] = blank
        dst[plane, pl.ds((height + 1) * padded, padded), :] = blank

    def one_block(block, carry):
        rows = jnp.swapaxes(load(pl.ds(pl.multiple_of(ROWS * block, ROWS), ROWS)), 0, 1)
        if padded != chans:
            fill = jnp.zeros((ROWS, padded - chans, width), F32)
            rows = jnp.concatenate([rows, fill], axis=1)
        hi, lo = split(rows.reshape(ROWS * padded, width))
        start = pl.multiple_of((ROWS * block + 1) * padded, padded)
        dst_hi[plane, pl.ds(start, ROWS * padded), :] = hi
        dst_lo[plane, pl.ds(start, ROWS * padded), :] = lo
        return carry

    lax.fori_loop(0, height // ROWS, one_block, 0, unroll=True)


def conv_kernel(dims, mode, sizes, unroll, counts, *refs):
    chans, padded, planes, height = dims
    ins, accs = counts
    weight, *fields = refs[:ins]
    acc = refs[ins] if accs else None
    results = refs[ins + accs : ins + accs + len(sizes)]
    xh, xl = refs[ins + accs + len(sizes) :]
    step = pl.program_id(0)
    width = xh.shape[-1]
    rows_out = sum(sizes)
    span = 3 * padded
    if mode == "outer":
        bit, d, active = fields[2], step * (planes - 1), None
    elif mode == "inner":
        bit, d, active = None, step - 1, step > 1
    else:
        bit, d, active = fields[3], step - 1, step > 0

    if bit is not None:
        sibling, neighbour = fields[:2] if mode == "outer" else fields[1:3]

        @pl.when(step == 0)
        def _():
            for ref, side in ((sibling, 1 - bit[0]), (neighbour, bit[0])):
                fill_plane(
                    xh,
                    xl,
                    side * (planes + 1),
                    lambda s, r=ref: r[:, 0, s, :],
                    chans,
                    padded,
                    height,
                )

    if mode != "outer":
        field = fields[0]

        @pl.when(step < planes)
        def _():
            fill_plane(xh, xl, step + 1, lambda s: field[:, 0, s, :], chans, padded, height)

    lane = lax.broadcasted_iota(jnp.int32, (rows_out, width), 1)
    first = lane == 0
    last = lane == width - 1

    def one_block(block, carry):
        h = ROWS * block
        parts = []
        for src in (xh, xl):
            for i in range(3):
                window = src[
                    d + i, pl.ds(pl.multiple_of(h * padded, padded), (ROWS + 2) * padded), :
                ]
                parts.append(
                    jnp.concatenate(
                        [window[r * padded : r * padded + span] for r in range(ROWS)], axis=1
                    )
                )
        parts = parts + parts[:3]
        extra = weight.shape[1] - 9 * span
        if extra:
            parts.append(jnp.zeros((extra, ROWS * width), BF16))
        y = jnp.dot(
            weight[...], jnp.concatenate(parts, axis=0), preferred_element_type=F32
        )
        rows = []
        for r in range(ROWS):
            z = y[:, r * width : (r + 1) * width]
            left = jnp.where(first, 0.0, pltpu.roll(z[:rows_out], 1, 1))
            right = jnp.where(last, 0.0, pltpu.roll(z[2 * rows_out :], width - 1, 1))
            rows.append(z[rows_out : 2 * rows_out] + left + right)
        swapped = jnp.swapaxes(jnp.stack(rows), 0, 1)
        where = pl.ds(pl.multiple_of(h, ROWS), ROWS)
        start = 0
        for ref, size in zip(results, sizes):
            piece = swapped[start : start + size]
            if acc is not None:
                piece = piece + acc[:, 0, where, :]
            ref[:, 0, where, :] = piece
            start += size
        return carry

    def plane_sums():
        lax.fori_loop(0, height // ROWS, one_block, 0, unroll=unroll)

    if active is None:
        plane_sums()
    else:
        pl.when(active)(plane_sums)


def conv(mode, fields, halo, weight, bit, sizes, unroll, acc=None, keep=False):
    width = fields[0].shape[-1]
    if mode == "outer":
        chans = halo[0].shape[0]
        planes, height = fields[0].shape[0] - 2, halo[0].shape[2]
    else:
        chans, planes, height, _ = fields[0].shape
    padded = up_to(chans, 16)
    held = (planes + 2, (height + 2) * padded, width)
    if mode == "outer":
        steps, out_planes = 2, 2
        plane_of, place_of = (lambda d: d * (planes - 1)), (lambda d: d)
    elif mode == "inner":
        steps, out_planes = planes, planes - 2
        plane_of = lambda d: jnp.maximum(d - 1, 1)
        place_of = lambda d: jnp.maximum(d - 2, 0)
    else:
        steps, out_planes = planes + 1, planes
        plane_of = place_of = lambda d: jnp.maximum(d - 1, 0)
    if acc is not None:
        out_planes, place_of = planes, plane_of

    def plane_spec(size):
        return pl.BlockSpec((size, 1, height, width), lambda d: (0, place_of(d), 0, 0))

    args, in_specs = [weight], [WHOLE]
    if mode != "outer":
        args.append(fields[0])
        in_specs.append(
            pl.BlockSpec(
                (chans, 1, height, width), lambda d: (0, jnp.minimum(d, planes - 1), 0, 0)
            )
        )
    if mode != "inner":
        args += [*halo, bit]
        in_specs += [WHOLE, WHOLE, SCALAR]
    ins = len(args)
    aliases = {}
    if acc is not None:
        aliases[ins] = 0
        args.append(acc)
        in_specs.append(plane_spec(sizes[0]))
    outs = [jax.ShapeDtypeStruct((size, out_planes, height, width), F32) for size in sizes]
    out_specs = [plane_spec(size) for size in sizes]
    scratch = []
    parts = [jax.ShapeDtypeStruct(held, BF16)] * 2
    if mode == "outer":
        for index in range(2):
            aliases[len(args)] = len(outs)
            args.append(fields[index])
            in_specs.append(WHOLE)
            outs.append(parts[index])
            out_specs.append(WHOLE)
    elif keep:
        outs += parts
        out_specs += [WHOLE] * 2
    else:
        scratch = [pltpu.VMEM(held, BF16)] * 2
    skip = 2 if mode == "outer" else 0
    accs = 0 if acc is None else 1

    def kernel(*refs):
        refs = refs[: ins + accs] + refs[ins + accs + skip :]
        conv_kernel(
            (chans, padded, planes, height), mode, sizes, unroll, (ins, accs), *refs
        )

    cells = planes * height * width
    return pl.pallas_call(
        kernel,
        grid=(steps,),
        in_specs=in_specs,
        out_specs=out_specs,
        out_shape=outs,
        scratch_shapes=scratch,
        input_output_aliases=aliases,
        compiler_params=params(),
        cost_estimate=pl.CostEstimate(
            flops=6 * 27 * chans * sum(sizes) * cells * 2 // COST_SHARE,
            bytes_accessed=4 * (chans + sum(sizes)) * cells // COST_SHARE,
            transcendentals=0,
        ),
        name="conv_" + mode,
    )(*args)


def grad_kernel(dims, others, *refs):
    padded, planes, height, width = dims
    xh, xl, cot, bit = refs[:4]
    done = refs[4 : 4 + others]
    *outs_refs, total = refs[4 + others :]
    outs = cot.shape[0]
    step = pl.program_id(0)
    span = 3 * padded
    half = 3 * span
    group = up_to(3 * outs, 128)

    @pl.when(step == 0)
    def _():
        total[...] = jnp.zeros_like(total)

    lane = lax.broadcasted_iota(jnp.int32, (outs, width), 1)
    first = lane == 0
    last = lane == width - 1
    lhs = []
    for src in (xh, xl):
        for i in range(3):
            window = src[step + i]
            lhs.append(
                jnp.concatenate(
                    [window[r * padded : r * padded + span] for r in range(height)], axis=1
                )
            )
    columns = []
    for block in range(height // ROWS):
        rows = jnp.swapaxes(cot[:, 0, pl.ds(ROWS * block, ROWS), :], 0, 1)
        for r in range(ROWS):
            c = rows[r]
            moved = [
                jnp.where(last, 0.0, pltpu.roll(c, width - 1, 1)),
                c,
                jnp.where(first, 0.0, pltpu.roll(c, 1, 1)),
            ]
            pieces = [split(m) for m in moved]
            gap = group - 3 * outs
            fill = [jnp.zeros((gap, width), BF16)] if gap else []
            columns.append(
                jnp.concatenate(
                    [p[0] for p in pieces] + fill + [p[1] for p in pieces] + fill, axis=0
                )
            )
    total[...] += lax.dot_general(
        jnp.concatenate(lhs, axis=0),
        jnp.concatenate(columns, axis=1),
        (((1,), (1,)), ((), ())),
        preferred_element_type=F32,
    )

    @pl.when(step == planes - 1)
    def _():
        summed = total[:half, :group] + total[:half, group:] + total[half:, :group]
        if len(outs_refs) == 1:
            outs_refs[0][...] = summed
        else:
            total[:half, :group] = summed
            rows = half // 2
            kept = pl.multiple_of(bit[0] * rows, 8)
            sent = pl.multiple_of((1 - bit[0]) * rows, 8)
            for ref, start in zip(outs_refs, (kept, sent)):
                for index, other in enumerate(done):
                    ref[index] = other[pl.ds(start, rows), :]
                ref[others] = total[pl.ds(start, rows), :group]


def kernel_grad(xh, xl, cot, bit, done=None):
    outs, planes, height, width = cot.shape
    padded = xh.shape[1] // (height + 2)
    group = up_to(3 * outs, 128)
    cells = planes * height * width
    rows = 9 * padded
    earlier = () if done is None else tuple(done)
    shape = (rows, group) if done is None else (len(earlier) + 1, rows // 2, group)
    shapes = [jax.ShapeDtypeStruct(shape, F32)] * (1 if done is None else 2)
    return pl.pallas_call(
        functools.partial(grad_kernel, (padded, planes, height, width), len(earlier)),
        grid=(planes,),
        in_specs=[WHOLE] * 2
        + [pl.BlockSpec((outs, 1, height, width), lambda d: (0, d, 0, 0)), SCALAR]
        + [WHOLE] * len(earlier),
        out_specs=[WHOLE] * len(shapes),
        out_shape=shapes,
        scratch_shapes=[pltpu.VMEM((2 * rows, 2 * group), F32)],
        compiler_params=params(),
        cost_estimate=pl.CostEstimate(
            flops=6 * 3 * rows * outs * cells * 2 // COST_SHARE,
            bytes_accessed=8 * outs * cells // COST_SHARE,
            transcendentals=0,
        ),
        name="kernel_grad",
    )(xh, xl, cot, bit, *earlier)


def three_parts(matrix, wide):
    hi, lo = split(matrix)
    parts = [hi, hi, lo]
    extra = wide - 3 * matrix.shape[1]
    if extra:
        parts.append(jnp.zeros((matrix.shape[0], extra), BF16))
    return jnp.concatenate(parts, axis=1)


def weight_kernel(groups, me, taps, forward, *refs):
    backward, turned = refs[:groups], refs[groups]
    cin, channels = taps.shape[1:]
    mine = channels // groups
    pad_in = up_to(cin, 16)
    pad_out = up_to(mine, 16)
    for k in range(3):
        blocks = []
        for tap in range(9):
            blocks.append(taps[3 * tap + k])
            if pad_in != cin:
                blocks.append(jnp.zeros((pad_in - cin, channels), F32))
        turned[...] = jnp.concatenate(blocks, axis=0).T
        for g in range(groups):
            owner = lax.rem(me[0] + g, groups)
            rows = turned[pl.ds(pl.multiple_of(owner * mine, mine), mine), :]
            forward[pl.ds(k * channels + g * mine, mine), :] = three_parts(
                rows, forward.shape[1]
            )
    for s in range(groups):
        owner = lax.rem(me[0] + s, groups)
        for k in range(3):
            blocks = []
            for tap in range(9):
                block = taps[26 - 3 * tap - k]
                chosen = block[:, :mine]
                for q in range(1, groups):
                    chosen = jnp.where(owner == q, block[:, q * mine : (q + 1) * mine], chosen)
                blocks.append(chosen)
                if pad_out != mine:
                    blocks.append(jnp.zeros((cin, pad_out - mine), F32))
            backward[s][pl.ds(k * cin, cin), :] = three_parts(
                jnp.concatenate(blocks, axis=1), backward[s].shape[1]
            )


def weight_matrices(me, taps, groups):
    _, cin, channels = taps.shape
    mine = channels // groups
    pad_in = up_to(cin, 16)
    wide_in = up_to(27 * pad_in, 128)
    wide_out = up_to(27 * up_to(mine, 16), 128)
    return pl.pallas_call(
        functools.partial(weight_kernel, groups),
        in_specs=[SCALAR, WHOLE],
        out_specs=[WHOLE] * (groups + 1),
        out_shape=[jax.ShapeDtypeStruct((3 * channels, wide_in), BF16)]
        + [jax.ShapeDtypeStruct((3 * cin, wide_out), BF16)] * groups,
        scratch_shapes=[pltpu.VMEM((channels, 9 * pad_in), F32)],
        compiler_params=params(0),
        name="weights",
    )(me, taps)


def finish_kernel(groups, scale, me, bit, mine_ref, other_ref, out):
    cin, channels = out.shape[1:]
    mine = channels // groups
    padded = 2 * mine_ref.shape[1] // 9
    low = bit[0] == 0
    totals = []
    for s in range(groups):
        a, b = mine_ref[s] * scale, other_ref[s] * scale
        totals.append(jnp.concatenate([jnp.where(low, a, b), jnp.where(low, b, a)], axis=0))
    for k in range(3):
        pieces = [t[:, k * mine : (k + 1) * mine] for t in totals]
        blocks = []
        for q in range(groups):
            source = lax.rem(q - me[0] + groups, groups)
            chosen = pieces[0]
            for s in range(1, groups):
                chosen = jnp.where(source == s, pieces[s], chosen)
            blocks.append(chosen)
        wide = jnp.concatenate(blocks, axis=1)
        for tap in range(9):
            out[3 * tap + k] = wide[tap * padded : tap * padded + cin]


def finish(me, bit, value, other, groups, cin, channels, scale):
    return pl.pallas_call(
        functools.partial(finish_kernel, groups, scale),
        in_specs=[SCALAR, SCALAR, WHOLE, WHOLE],
        out_specs=WHOLE,
        out_shape=jax.ShapeDtypeStruct((27, cin, channels), F32),
        compiler_params=params(0),
        name="finish",
    )(me, bit, value, other)


def add_kernel(count, *refs):
    total = refs[0][...]
    for ref in refs[1:count]:
        total = total + ref[...]
    refs[-1][...] = total


def add_pieces(own, pieces, whole, shape, first, block, plane_of):
    channels, out_planes, height, width = pieces[0].shape
    size = (block, 1, height, width)
    start = first // block
    here = pl.BlockSpec(size, lambda p, c: (c, p, 0, 0))
    args = [own, *pieces]
    specs = [pl.BlockSpec(size, lambda p, c: (start + c, p, 0, 0))] + [here] * len(pieces)
    aliases = {}
    if whole is not None:
        aliases[len(args)] = 0
        args.append(whole)
        specs.append(pl.BlockSpec(memory_space=pl.ANY))
    return pl.pallas_call(
        functools.partial(add_kernel, 1 + len(pieces)),
        grid=(out_planes, channels // block),
        in_specs=specs,
        out_specs=pl.BlockSpec(size, lambda p, c: (start + c, plane_of(p), 0, 0)),
        out_shape=jax.ShapeDtypeStruct(shape, F32),
        input_output_aliases=aliases,
        compiler_params=params(2),
        cost_estimate=pl.CostEstimate(
            flops=pieces[0].size, bytes_accessed=12 * pieces[0].size, transcendentals=0
        ),
        name="add_pieces",
    )(*args)


def cut_edges(field, bit):
    ends = field.shape[1] - 1
    to_sibling = lax.dynamic_slice_in_dim(field, (1 - bit[0]) * ends, 1, axis=1)
    to_neighbour = lax.dynamic_slice_in_dim(field, bit[0] * ends, 1, axis=1)
    return lax.optimization_barrier((field, to_sibling, to_neighbour))


def slab_halo(to_sibling, to_neighbour):
    count = lax.axis_size("slab")
    across = [(i, i + 1) for i in range(1, count - 1, 2)]
    across += [(j, i) for i, j in across]
    return slab_swap(to_sibling, 1), lax.ppermute(to_neighbour, "slab", across)


def slab_swap(value, bit):
    return lax.ppermute(
        value, "slab", [(i, i ^ bit) for i in range(lax.axis_size("slab"))]
    )


def per_device(activations, kernel, cotangent):
    groups = lax.axis_size("chan")
    slabs = lax.axis_size("slab")
    assert slabs >= 16 and slabs & (slabs - 1) == 0 and groups > 1
    me = lax.axis_index("chan").reshape(1)
    bit = lax.rem(lax.axis_index("slab"), 2).reshape(1)
    channels, taps, cin = kernel.shape
    mine = channels // groups
    planes, height, width = activations.shape[1:]
    quarter = mine // 4
    pieces = (mine - 2 * quarter, quarter, quarter)
    after = lax.optimization_barrier

    cots = [cotangent]
    for s in range(1, groups):
        cots.append(
            lax.ppermute(cotangent, "chan", [((i + s) % groups, i) for i in range(groups)])
        )
    activations, *edges = cut_edges(activations, bit)
    act_halo = slab_halo(*edges)
    forward, *backward = weight_matrices(me, kernel.transpose(1, 2, 0), groups)

    own_inner, *inner, xh, xl = conv(
        "inner", [activations], None, forward, bit, (mine,) * groups, 2, keep=True
    )
    own, xh, *act_halo = after((cotangent, xh, *act_halo))
    own, *edges = cut_edges(own, bit)
    *edges, xh = after((*edges, xh))
    cot_halo = slab_halo(*edges)
    own_outer, *outer, xh, xl = conv(
        "outer", [xh, xl], act_halo, forward, bit, (mine,) + pieces * (groups - 1), 2
    )

    def to_owner(part, s):
        return lax.ppermute(part, "chan", [(i, (i + s) % groups) for i in range(groups)])

    got_inner = [to_owner(inner[s - 1], s) for s in range(1, groups)]
    got_outer = []
    for index in range(len(pieces)):
        parts = outer[index :: len(pieces)]
        got_outer.append([to_owner(parts[s - 1], s) for s in range(1, groups)])

    grads = list(kernel_grad(xh, xl, own, bit))
    (input_grad,) = conv("all", [own], cot_halo, backward[0], bit, (cin,), 4)
    for s in range(1, groups):
        cot, input_grad, *grads = after((cots[s], input_grad, *grads))
        cot, *edges = cut_edges(cot, bit)
        halo = slab_halo(*edges)
        if s < groups - 1:
            grads += kernel_grad(xh, xl, cot, bit)
        else:
            kept, sent = kernel_grad(xh, xl, cot, bit, grads)
            value = kept + slab_swap(sent, 1)
            value, cot = after((value, cot))
            other = slab_swap(value, 2)
        input_grad, ch, cl = conv(
            "inner", [cot], None, backward[s], bit, (cin,), 4, input_grad, keep=True
        )
        if s == groups - 1:
            other, ch, *halo = after((other, ch, *halo))
            value = value + other
            other = slab_swap(value, 4)
        input_grad, _, _ = conv(
            "outer", [ch, cl], halo, backward[s], bit, (cin,), 4, input_grad
        )

    other, input_grad = after((other, input_grad))
    value = value + other
    step = 8
    while step < slabs // 2:
        value = value + slab_swap(value, step)
        step *= 2
    *got_inner, value = after((*got_inner, value))
    other = slab_swap(value, step)
    features = add_pieces(
        own_inner, got_inner, None, (mine, planes, height, width), 0,
        mine // 2, lambda p: p + 1,
    )
    other, features = after((other, features))
    value = value + other
    cells_all = planes * slabs * height * width
    weight_grad = finish(
        me, bit, value, slab_swap(value, 1), groups, cin, channels, 1.0 / math.sqrt(cells_all)
    )
    weight_grad, features = after((weight_grad, features))
    first = 0
    for got, size in zip(got_outer, pieces):
        *got, features = after((*got, features))
        features = add_pieces(
            own_outer, got, features, features.shape, first, size,
            lambda p: p * (planes - 1),
        )
        first += size
    return features, input_grad, weight_grad.transpose(2, 0, 1)


def solution(mesh):
    return jax.shard_map(
        per_device,
        mesh=mesh,
        in_specs=(
            P("chan", "slab", None, None),
            P(None, None, "chan"),
            P("chan", "slab", None, None),
        ),
        out_specs=(
            P("chan", "slab", None, None),
            P("chan", "slab", None, None),
            P(None, None, "chan"),
        ),
        check_vma=False,
    )
```

```python
import functools
import math

import jax
import jax.numpy as jnp
from jax import lax
from jax.experimental import pallas as pl
from jax.experimental.pallas import tpu as pltpu
from jax.sharding import PartitionSpec as P

F32 = jnp.float32
BF16 = jnp.bfloat16
ROWS = 8
VMEM_LIMIT = 16 << 20
COST_SHARE = 20
WHOLE = pl.BlockSpec(memory_space=pltpu.VMEM)
SCALAR = pl.BlockSpec(memory_space=pltpu.SMEM)


def up_to(size, unit):
    return -(-size // unit) * unit


def split(x):
    hi = x.astype(BF16)
    return hi, (x - hi.astype(F32)).astype(BF16)


def params(steps=1):
    return pltpu.CompilerParams(
        dimension_semantics=("arbitrary",) * steps or None, vmem_limit_bytes=VMEM_LIMIT
    )


def fill_plane(dst_hi, dst_lo, plane, load, chans, padded, height):
    width = dst_hi.shape[-1]
    blank = jnp.zeros((padded, width), BF16)
    for dst in (dst_hi, dst_lo):
        dst[plane, pl.ds(0, padded), :] = blank
        dst[plane, pl.ds((height + 1) * padded, padded), :] = blank

    def one_block(block, carry):
        rows = jnp.swapaxes(load(pl.ds(pl.multiple_of(ROWS * block, ROWS), ROWS)), 0, 1)
        if padded != chans:
            fill = jnp.zeros((ROWS, padded - chans, width), F32)
            rows = jnp.concatenate([rows, fill], axis=1)
        hi, lo = split(rows.reshape(ROWS * padded, width))
        start = pl.multiple_of((ROWS * block + 1) * padded, padded)
        dst_hi[plane, pl.ds(start, ROWS * padded), :] = hi
        dst_lo[plane, pl.ds(start, ROWS * padded), :] = lo
        return carry

    lax.fori_loop(0, height // ROWS, one_block, 0, unroll=True)


def conv_kernel(dims, mode, sizes, unroll, counts, *refs):
    chans, padded, planes, height = dims
    ins, accs = counts
    weight, *fields = refs[:ins]
    acc = refs[ins] if accs else None
    results = refs[ins + accs : ins + accs + len(sizes)]
    xh, xl = refs[ins + accs + len(sizes) :]
    step = pl.program_id(0)
    width = xh.shape[-1]
    rows_out = sum(sizes)
    span = 3 * padded
    if mode == "outer":
        bit, d, active = fields[2], step * (planes - 1), None
    elif mode == "inner":
        bit, d, active = None, step - 1, step > 1
    else:
        bit, d, active = fields[3], step - 1, step > 0

    if bit is not None:
        sibling, neighbour = fields[:2] if mode == "outer" else fields[1:3]

        @pl.when(step == 0)
        def _():
            for ref, side in ((sibling, 1 - bit[0]), (neighbour, bit[0])):
                fill_plane(
                    xh,
                    xl,
                    side * (planes + 1),
                    lambda s, r=ref: r[:, 0, s, :],
                    chans,
                    padded,
                    height,
                )

    if mode != "outer":
        field = fields[0]

        @pl.when(step < planes)
        def _():
            fill_plane(xh, xl, step + 1, lambda s: field[:, 0, s, :], chans, padded, height)

    lane = lax.broadcasted_iota(jnp.int32, (rows_out, width), 1)
    first = lane == 0
    last = lane == width - 1

    def one_block(block, carry):
        h = ROWS * block
        parts = []
        for src in (xh, xl):
            for i in range(3):
                window = src[
                    d + i, pl.ds(pl.multiple_of(h * padded, padded), (ROWS + 2) * padded), :
                ]
                parts.append(
                    jnp.concatenate(
                        [window[r * padded : r * padded + span] for r in range(ROWS)], axis=1
                    )
                )
        parts = parts + parts[:3]
        extra = weight.shape[1] - 9 * span
        if extra:
            parts.append(jnp.zeros((extra, ROWS * width), BF16))
        y = jnp.dot(
            weight[...], jnp.concatenate(parts, axis=0), preferred_element_type=F32
        )
        rows = []
        for r in range(ROWS):
            z = y[:, r * width : (r + 1) * width]
            left = jnp.where(first, 0.0, pltpu.roll(z[:rows_out], 1, 1))
            right = jnp.where(last, 0.0, pltpu.roll(z[2 * rows_out :], width - 1, 1))
            rows.append(z[rows_out : 2 * rows_out] + left + right)
        swapped = jnp.swapaxes(jnp.stack(rows), 0, 1)
        where = pl.ds(pl.multiple_of(h, ROWS), ROWS)
        start = 0
        for ref, size in zip(results, sizes):
            piece = swapped[start : start + size]
            if acc is not None:
                piece = piece + acc[:, 0, where, :]
            ref[:, 0, where, :] = piece
            start += size
        return carry

    def plane_sums():
        lax.fori_loop(0, height // ROWS, one_block, 0, unroll=unroll)

    if active is None:
        plane_sums()
    else:
        pl.when(active)(plane_sums)


def conv(mode, fields, halo, weight, bit, sizes, unroll, acc=None, keep=False):
    width = fields[0].shape[-1]
    if mode == "outer":
        chans = halo[0].shape[0]
        planes, height = fields[0].shape[0] - 2, halo[0].shape[2]
    else:
        chans, planes, height, _ = fields[0].shape
    padded = up_to(chans, 16)
    held = (planes + 2, (height + 2) * padded, width)
    if mode == "outer":
        steps, out_planes = 2, 2
        plane_of, place_of = (lambda d: d * (planes - 1)), (lambda d: d)
    elif mode == "inner":
        steps, out_planes = planes, planes - 2
        plane_of = lambda d: jnp.maximum(d - 1, 1)
        place_of = lambda d: jnp.maximum(d - 2, 0)
    else:
        steps, out_planes = planes + 1, planes
        plane_of = place_of = lambda d: jnp.maximum(d - 1, 0)
    if acc is not None:
        out_planes, place_of = planes, plane_of

    def plane_spec(size):
        return pl.BlockSpec((size, 1, height, width), lambda d: (0, place_of(d), 0, 0))

    args, in_specs = [weight], [WHOLE]
    if mode != "outer":
        args.append(fields[0])
        in_specs.append(
            pl.BlockSpec(
                (chans, 1, height, width), lambda d: (0, jnp.minimum(d, planes - 1), 0, 0)
            )
        )
    if mode != "inner":
        args += [*halo, bit]
        in_specs += [WHOLE, WHOLE, SCALAR]
    ins = len(args)
    aliases = {}
    if acc is not None:
        aliases[ins] = 0
        args.append(acc)
        in_specs.append(plane_spec(sizes[0]))
    outs = [jax.ShapeDtypeStruct((size, out_planes, height, width), F32) for size in sizes]
    out_specs = [plane_spec(size) for size in sizes]
    scratch = []
    parts = [jax.ShapeDtypeStruct(held, BF16)] * 2
    if mode == "outer":
        for index in range(2):
            aliases[len(args)] = len(outs)
            args.append(fields[index])
            in_specs.append(WHOLE)
            outs.append(parts[index])
            out_specs.append(WHOLE)
    elif keep:
        outs += parts
        out_specs += [WHOLE] * 2
    else:
        scratch = [pltpu.VMEM(held, BF16)] * 2
    skip = 2 if mode == "outer" else 0
    accs = 0 if acc is None else 1

    def kernel(*refs):
        refs = refs[: ins + accs] + refs[ins + accs + skip :]
        conv_kernel(
            (chans, padded, planes, height), mode, sizes, unroll, (ins, accs), *refs
        )

    cells = planes * height * width
    return pl.pallas_call(
        kernel,
        grid=(steps,),
        in_specs=in_specs,
        out_specs=out_specs,
        out_shape=outs,
        scratch_shapes=scratch,
        input_output_aliases=aliases,
        compiler_params=params(),
        cost_estimate=pl.CostEstimate(
            flops=6 * 27 * chans * sum(sizes) * cells * 2 // COST_SHARE,
            bytes_accessed=4 * (chans + sum(sizes)) * cells // COST_SHARE,
            transcendentals=0,
        ),
        name="conv_" + mode,
    )(*args)


def grad_kernel(dims, others, *refs):
    padded, planes, height, width = dims
    xh, xl, cot, bit = refs[:4]
    done = refs[4 : 4 + others]
    *outs_refs, total = refs[4 + others :]
    outs = cot.shape[0]
    step = pl.program_id(0)
    span = 3 * padded
    half = 3 * span
    group = up_to(3 * outs, 128)

    @pl.when(step == 0)
    def _():
        total[...] = jnp.zeros_like(total)

    lane = lax.broadcasted_iota(jnp.int32, (outs, width), 1)
    first = lane == 0
    last = lane == width - 1
    lhs = []
    for src in (xh, xl):
        for i in range(3):
            window = src[step + i]
            lhs.append(
                jnp.concatenate(
                    [window[r * padded : r * padded + span] for r in range(height)], axis=1
                )
            )
    columns = []
    for block in range(height // ROWS):
        rows = jnp.swapaxes(cot[:, 0, pl.ds(ROWS * block, ROWS), :], 0, 1)
        for r in range(ROWS):
            c = rows[r]
            moved = [
                jnp.where(last, 0.0, pltpu.roll(c, width - 1, 1)),
                c,
                jnp.where(first, 0.0, pltpu.roll(c, 1, 1)),
            ]
            pieces = [split(m) for m in moved]
            gap = group - 3 * outs
            fill = [jnp.zeros((gap, width), BF16)] if gap else []
            columns.append(
                jnp.concatenate(
                    [p[0] for p in pieces] + fill + [p[1] for p in pieces] + fill, axis=0
                )
            )
    total[...] += lax.dot_general(
        jnp.concatenate(lhs, axis=0),
        jnp.concatenate(columns, axis=1),
        (((1,), (1,)), ((), ())),
        preferred_element_type=F32,
    )

    @pl.when(step == planes - 1)
    def _():
        summed = total[:half, :group] + total[:half, group:] + total[half:, :group]
        if len(outs_refs) == 1:
            outs_refs[0][...] = summed
        else:
            total[:half, :group] = summed
            rows = half // 2
            kept = pl.multiple_of(bit[0] * rows, 8)
            sent = pl.multiple_of((1 - bit[0]) * rows, 8)
            for ref, start in zip(outs_refs, (kept, sent)):
                for index, other in enumerate(done):
                    ref[index] = other[pl.ds(start, rows), :]
                ref[others] = total[pl.ds(start, rows), :group]


def kernel_grad(xh, xl, cot, bit, done=None):
    outs, planes, height, width = cot.shape
    padded = xh.shape[1] // (height + 2)
    group = up_to(3 * outs, 128)
    cells = planes * height * width
    rows = 9 * padded
    earlier = () if done is None else tuple(done)
    shape = (rows, group) if done is None else (len(earlier) + 1, rows // 2, group)
    shapes = [jax.ShapeDtypeStruct(shape, F32)] * (1 if done is None else 2)
    return pl.pallas_call(
        functools.partial(grad_kernel, (padded, planes, height, width), len(earlier)),
        grid=(planes,),
        in_specs=[WHOLE] * 2
        + [pl.BlockSpec((outs, 1, height, width), lambda d: (0, d, 0, 0)), SCALAR]
        + [WHOLE] * len(earlier),
        out_specs=[WHOLE] * len(shapes),
        out_shape=shapes,
        scratch_shapes=[pltpu.VMEM((2 * rows, 2 * group), F32)],
        compiler_params=params(),
        cost_estimate=pl.CostEstimate(
            flops=6 * 3 * rows * outs * cells * 2 // COST_SHARE,
            bytes_accessed=8 * outs * cells // COST_SHARE,
            transcendentals=0,
        ),
        name="kernel_grad",
    )(xh, xl, cot, bit, *earlier)


def three_parts(matrix, wide):
    hi, lo = split(matrix)
    parts = [hi, hi, lo]
    extra = wide - 3 * matrix.shape[1]
    if extra:
        parts.append(jnp.zeros((matrix.shape[0], extra), BF16))
    return jnp.concatenate(parts, axis=1)


def weight_kernel(groups, me, taps, forward, *refs):
    backward, turned = refs[:groups], refs[groups]
    cin, channels = taps.shape[1:]
    mine = channels // groups
    pad_in = up_to(cin, 16)
    pad_out = up_to(mine, 16)
    for k in range(3):
        blocks = []
        for tap in range(9):
            blocks.append(taps[3 * tap + k])
            if pad_in != cin:
                blocks.append(jnp.zeros((pad_in - cin, channels), F32))
        turned[...] = jnp.concatenate(blocks, axis=0).T
        for g in range(groups):
            owner = lax.rem(me[0] + g, groups)
            rows = turned[pl.ds(pl.multiple_of(owner * mine, mine), mine), :]
            forward[pl.ds(k * channels + g * mine, mine), :] = three_parts(
                rows, forward.shape[1]
            )
    for s in range(groups):
        owner = lax.rem(me[0] + s, groups)
        for k in range(3):
            blocks = []
            for tap in range(9):
                block = taps[26 - 3 * tap - k]
                chosen = block[:, :mine]
                for q in range(1, groups):
                    chosen = jnp.where(owner == q, block[:, q * mine : (q + 1) * mine], chosen)
                blocks.append(chosen)
                if pad_out != mine:
                    blocks.append(jnp.zeros((cin, pad_out - mine), F32))
            backward[s][pl.ds(k * cin, cin), :] = three_parts(
                jnp.concatenate(blocks, axis=1), backward[s].shape[1]
            )


def weight_matrices(me, taps, groups):
    _, cin, channels = taps.shape
    mine = channels // groups
    pad_in = up_to(cin, 16)
    wide_in = up_to(27 * pad_in, 128)
    wide_out = up_to(27 * up_to(mine, 16), 128)
    return pl.pallas_call(
        functools.partial(weight_kernel, groups),
        in_specs=[SCALAR, WHOLE],
        out_specs=[WHOLE] * (groups + 1),
        out_shape=[jax.ShapeDtypeStruct((3 * channels, wide_in), BF16)]
        + [jax.ShapeDtypeStruct((3 * cin, wide_out), BF16)] * groups,
        scratch_shapes=[pltpu.VMEM((channels, 9 * pad_in), F32)],
        compiler_params=params(0),
        name="weights",
    )(me, taps)


def finish_kernel(groups, scale, me, bit, mine_ref, other_ref, out):
    cin, channels = out.shape[1:]
    mine = channels // groups
    padded = 2 * mine_ref.shape[1] // 9
    low = bit[0] == 0
    totals = []
    for s in range(groups):
        a, b = mine_ref[s] * scale, other_ref[s] * scale
        totals.append(jnp.concatenate([jnp.where(low, a, b), jnp.where(low, b, a)], axis=0))
    for k in range(3):
        pieces = [t[:, k * mine : (k + 1) * mine] for t in totals]
        blocks = []
        for q in range(groups):
            source = lax.rem(q - me[0] + groups, groups)
            chosen = pieces[0]
            for s in range(1, groups):
                chosen = jnp.where(source == s, pieces[s], chosen)
            blocks.append(chosen)
        wide = jnp.concatenate(blocks, axis=1)
        for tap in range(9):
            out[3 * tap + k] = wide[tap * padded : tap * padded + cin]


def finish(me, bit, value, other, groups, cin, channels, scale):
    return pl.pallas_call(
        functools.partial(finish_kernel, groups, scale),
        in_specs=[SCALAR, SCALAR, WHOLE, WHOLE],
        out_specs=WHOLE,
        out_shape=jax.ShapeDtypeStruct((27, cin, channels), F32),
        compiler_params=params(0),
        name="finish",
    )(me, bit, value, other)


def add_kernel(count, *refs):
    total = refs[0][...]
    for ref in refs[1:count]:
        total = total + ref[...]
    refs[-1][...] = total


def add_pieces(own, pieces, whole, shape, first, block, plane_of):
    channels, out_planes, height, width = pieces[0].shape
    size = (block, 1, height, width)
    start = first // block
    here = pl.BlockSpec(size, lambda p, c: (c, p, 0, 0))
    args = [own, *pieces]
    specs = [pl.BlockSpec(size, lambda p, c: (start + c, p, 0, 0))] + [here] * len(pieces)
    aliases = {}
    if whole is not None:
        aliases[len(args)] = 0
        args.append(whole)
        specs.append(pl.BlockSpec(memory_space=pl.ANY))
    return pl.pallas_call(
        functools.partial(add_kernel, 1 + len(pieces)),
        grid=(out_planes, channels // block),
        in_specs=specs,
        out_specs=pl.BlockSpec(size, lambda p, c: (start + c, plane_of(p), 0, 0)),
        out_shape=jax.ShapeDtypeStruct(shape, F32),
        input_output_aliases=aliases,
        compiler_params=params(2),
        cost_estimate=pl.CostEstimate(
            flops=pieces[0].size, bytes_accessed=12 * pieces[0].size, transcendentals=0
        ),
        name="add_pieces",
    )(*args)


def cut_edges(field, bit):
    ends = field.shape[1] - 1
    to_sibling = lax.dynamic_slice_in_dim(field, (1 - bit[0]) * ends, 1, axis=1)
    to_neighbour = lax.dynamic_slice_in_dim(field, bit[0] * ends, 1, axis=1)
    return lax.optimization_barrier((field, to_sibling, to_neighbour))


def slab_halo(to_sibling, to_neighbour):
    count = lax.axis_size("slab")
    across = [(i, i + 1) for i in range(1, count - 1, 2)]
    across += [(j, i) for i, j in across]
    return slab_swap(to_sibling, 1), lax.ppermute(to_neighbour, "slab", across)


def slab_swap(value, bit):
    return lax.ppermute(
        value, "slab", [(i, i ^ bit) for i in range(lax.axis_size("slab"))]
    )


def per_device(activations, kernel, cotangent):
    groups = lax.axis_size("chan")
    slabs = lax.axis_size("slab")
    assert slabs >= 16 and slabs & (slabs - 1) == 0 and groups > 1
    me = lax.axis_index("chan").reshape(1)
    bit = lax.rem(lax.axis_index("slab"), 2).reshape(1)
    channels, taps, cin = kernel.shape
    mine = channels // groups
    planes, height, width = activations.shape[1:]

    quarter = max(mine // 4, 1)
    pieces = (mine - quarter, quarter)
    after = lax.optimization_barrier

    cots = [cotangent]
    for s in range(1, groups):
        cots.append(
            lax.ppermute(cotangent, "chan", [((i + s) % groups, i) for i in range(groups)])
        )
    activations, *edges = cut_edges(activations, bit)
    act_halo = slab_halo(*edges)
    forward, *backward = weight_matrices(me, kernel.transpose(1, 2, 0), groups)

    own_inner, *inner, xh, xl = conv(
        "inner", [activations], None, forward, bit, (mine,) * groups, 2, keep=True
    )
    own, xh, *act_halo = after((cotangent, xh, *act_halo))
    own, *edges = cut_edges(own, bit)
    *edges, xh = after((*edges, xh))
    cot_halo = slab_halo(*edges)
    own_outer, *outer, xh, xl = conv(
        "outer", [xh, xl], act_halo, forward, bit, (mine,) + pieces * (groups - 1), 2
    )

    def to_owner(part, s):
        return lax.ppermute(part, "chan", [(i, (i + s) % groups) for i in range(groups)])

    got_inner = [to_owner(inner[s - 1], s) for s in range(1, groups)]
    got_outer = []
    for index in range(len(pieces)):
        parts = outer[index :: len(pieces)]
        got_outer.append([to_owner(parts[s - 1], s) for s in range(1, groups)])

    grads = list(kernel_grad(xh, xl, own, bit))
    (input_grad,) = conv("all", [own], cot_halo, backward[0], bit, (cin,), 4)
    for s in range(1, groups):
        cot, input_grad, *grads = after((cots[s], input_grad, *grads))
        cot, *edges = cut_edges(cot, bit)
        halo = slab_halo(*edges)
        if s < groups - 1:
            grads += kernel_grad(xh, xl, cot, bit)
        else:
            kept, sent = kernel_grad(xh, xl, cot, bit, grads)
            value = kept + slab_swap(sent, 1)
            value, cot = after((value, cot))
            other = slab_swap(value, 2)
        input_grad, ch, cl = conv(
            "inner", [cot], None, backward[s], bit, (cin,), 4, input_grad, keep=True
        )
        if s == groups - 1:
            other, ch, *halo = after((other, ch, *halo))
            value = value + other
            other = slab_swap(value, 4)
        input_grad, _, _ = conv(
            "outer", [ch, cl], halo, backward[s], bit, (cin,), 4, input_grad
        )

    other, input_grad = after((other, input_grad))
    value = value + other
    step = 8
    while step < slabs // 2:
        value = value + slab_swap(value, step)
        step *= 2
    *got_inner, value = after((*got_inner, value))
    other = slab_swap(value, step)
    features = add_pieces(
        own_inner, got_inner, None, (mine, planes, height, width), 0,
        mine // 2, lambda p: p + 1,
    )
    other, features = after((other, features))
    value = value + other
    cells_all = planes * slabs * height * width
    weight_grad = finish(
        me, bit, value, slab_swap(value, 1), groups, cin, channels, 1.0 / math.sqrt(cells_all)
    )
    weight_grad, features = after((weight_grad, features))
    first = 0
    for got, size in zip(got_outer, pieces):
        *got, features = after((*got, features))
        features = add_pieces(
            own_outer, got, features, features.shape, first, size,
            lambda p: p * (planes - 1),
        )
        first += size
    return features, input_grad, weight_grad.transpose(2, 0, 1)


def solution(mesh):
    return jax.shard_map(
        per_device,
        mesh=mesh,
        in_specs=(
            P("chan", "slab", None, None),
            P(None, None, "chan"),
            P("chan", "slab", None, None),
        ),
        out_specs=(
            P("chan", "slab", None, None),
            P("chan", "slab", None, None),
            P(None, None, "chan"),
        ),
        check_vma=False,
    )
```

```python
import functools
import math

import jax
import jax.numpy as jnp
from jax import lax
from jax.experimental import pallas as pl
from jax.experimental.pallas import tpu as pltpu
from jax.sharding import PartitionSpec as P

F32 = jnp.float32
BF16 = jnp.bfloat16
ROWS = 8
VMEM_LIMIT = 16 << 20
COST_SHARE = 20
WHOLE = pl.BlockSpec(memory_space=pltpu.VMEM)
SCALAR = pl.BlockSpec(memory_space=pltpu.SMEM)


def up_to(size, unit):
    return -(-size // unit) * unit


def split(x):
    hi = x.astype(BF16)
    return hi, (x - hi.astype(F32)).astype(BF16)


def params(steps=1):
    return pltpu.CompilerParams(
        dimension_semantics=("arbitrary",) * steps or None, vmem_limit_bytes=VMEM_LIMIT
    )


def fill_plane(dst_hi, dst_lo, plane, load, chans, padded, height):
    width = dst_hi.shape[-1]
    blank = jnp.zeros((padded, width), BF16)
    for dst in (dst_hi, dst_lo):
        dst[plane, pl.ds(0, padded), :] = blank
        dst[plane, pl.ds((height + 1) * padded, padded), :] = blank

    def one_block(block, carry):
        rows = jnp.swapaxes(load(pl.ds(pl.multiple_of(ROWS * block, ROWS), ROWS)), 0, 1)
        if padded != chans:
            fill = jnp.zeros((ROWS, padded - chans, width), F32)
            rows = jnp.concatenate([rows, fill], axis=1)
        hi, lo = split(rows.reshape(ROWS * padded, width))
        start = pl.multiple_of((ROWS * block + 1) * padded, padded)
        dst_hi[plane, pl.ds(start, ROWS * padded), :] = hi
        dst_lo[plane, pl.ds(start, ROWS * padded), :] = lo
        return carry

    lax.fori_loop(0, height // ROWS, one_block, 0, unroll=True)


def conv_kernel(dims, mode, sizes, unroll, counts, inner, *refs):
    chans, padded, planes, height = dims
    ins, accs = counts
    weight, *fields = refs[:ins]
    acc = refs[ins] if accs else None
    results = refs[ins + accs : ins + accs + len(sizes)]
    xh, xl = refs[ins + accs + len(sizes) :][:2]
    step = pl.program_id(0)
    width = xh.shape[-1]
    rows_out = sum(sizes)
    span = 3 * padded
    if mode == "outer":
        bit, d, active = fields[2], step * (planes - 1), None
    elif mode == "inner":
        bit, d, active = None, step - 1, step > 1
    else:
        bit, d, active = fields[3], step - 1, step > 0

    if bit is not None:
        sibling, neighbour = fields[:2] if mode == "outer" else fields[1:3]

        @pl.when(step == 0)
        def _():
            for src, dst in zip(inner, (xh, xl)):
                for plane in range(1, planes + 1):
                    dst[plane] = src[plane]
            for ref, side in ((sibling, 1 - bit[0]), (neighbour, bit[0])):
                fill_plane(
                    xh,
                    xl,
                    side * (planes + 1),
                    lambda s, r=ref: r[:, 0, s, :],
                    chans,
                    padded,
                    height,
                )

    if mode != "outer":
        field = fields[0]

        @pl.when(step < planes)
        def _():
            fill_plane(xh, xl, step + 1, lambda s: field[:, 0, s, :], chans, padded, height)

    lane = lax.broadcasted_iota(jnp.int32, (rows_out, width), 1)
    first = lane == 0
    last = lane == width - 1

    def one_block(block, carry):
        h = ROWS * block
        parts = []
        for src in (xh, xl):
            for i in range(3):
                window = src[
                    d + i, pl.ds(pl.multiple_of(h * padded, padded), (ROWS + 2) * padded), :
                ]
                parts.append(
                    jnp.concatenate(
                        [window[r * padded : r * padded + span] for r in range(ROWS)], axis=1
                    )
                )
        parts = parts + parts[:3]
        extra = weight.shape[1] - 9 * span
        if extra:
            parts.append(jnp.zeros((extra, ROWS * width), BF16))
        y = jnp.dot(
            weight[...], jnp.concatenate(parts, axis=0), preferred_element_type=F32
        )
        rows = []
        for r in range(ROWS):
            z = y[:, r * width : (r + 1) * width]
            left = jnp.where(first, 0.0, pltpu.roll(z[:rows_out], 1, 1))
            right = jnp.where(last, 0.0, pltpu.roll(z[2 * rows_out :], width - 1, 1))
            rows.append(z[rows_out : 2 * rows_out] + left + right)
        swapped = jnp.swapaxes(jnp.stack(rows), 0, 1)
        where = pl.ds(pl.multiple_of(h, ROWS), ROWS)
        start = 0
        for ref, size in zip(results, sizes):
            piece = swapped[start : start + size]
            if acc is not None:
                piece = piece + acc[:, 0, where, :]
            ref[:, 0, where, :] = piece
            start += size
        return carry

    def plane_sums():
        lax.fori_loop(0, height // ROWS, one_block, 0, unroll=unroll)

    if active is None:
        plane_sums()
    else:
        pl.when(active)(plane_sums)


def conv(mode, fields, halo, weight, bit, sizes, unroll, acc=None, keep=False):
    width = fields[0].shape[-1]
    if mode == "outer":
        chans = halo[0].shape[0]
        planes, height = fields[0].shape[0] - 2, halo[0].shape[2]
    else:
        chans, planes, height, _ = fields[0].shape
    padded = up_to(chans, 16)
    held = (planes + 2, (height + 2) * padded, width)
    if mode == "outer":
        steps, out_planes = 2, 2
        plane_of, place_of = (lambda d: d * (planes - 1)), (lambda d: d)
    elif mode == "inner":
        steps, out_planes = planes, planes - 2
        plane_of = lambda d: jnp.maximum(d - 1, 1)
        place_of = lambda d: jnp.maximum(d - 2, 0)
    else:
        steps, out_planes = planes + 1, planes
        plane_of = place_of = lambda d: jnp.maximum(d - 1, 0)
    if acc is not None:
        out_planes, place_of = planes, plane_of

    def plane_spec(size):
        return pl.BlockSpec((size, 1, height, width), lambda d: (0, place_of(d), 0, 0))

    args, in_specs = [weight], [WHOLE]
    if mode != "outer":
        args.append(fields[0])
        in_specs.append(
            pl.BlockSpec(
                (chans, 1, height, width), lambda d: (0, jnp.minimum(d, planes - 1), 0, 0)
            )
        )
    if mode != "inner":
        args += [*halo, bit]
        in_specs += [WHOLE, WHOLE, SCALAR]
    ins = len(args)
    aliases = {}
    if acc is not None:
        aliases[ins] = 0
        args.append(acc)
        in_specs.append(plane_spec(sizes[0]))
    outs = [jax.ShapeDtypeStruct((size, out_planes, height, width), F32) for size in sizes]
    out_specs = [plane_spec(size) for size in sizes]
    scratch = []
    parts = [jax.ShapeDtypeStruct(held, BF16)] * 2
    skip = 2 if mode == "outer" else 0
    if skip:
        args += fields
        in_specs += [WHOLE] * 2
    if keep:
        outs += parts
        out_specs += [WHOLE] * 2
    else:
        scratch = [pltpu.VMEM(held, BF16)] * 2
    accs = 0 if acc is None else 1

    def kernel(*refs):
        inner = refs[ins + accs : ins + accs + skip]
        refs = refs[: ins + accs] + refs[ins + accs + skip :]
        conv_kernel(
            (chans, padded, planes, height), mode, sizes, unroll, (ins, accs), inner, *refs
        )

    cells = planes * height * width
    return pl.pallas_call(
        kernel,
        grid=(steps,),
        in_specs=in_specs,
        out_specs=out_specs,
        out_shape=outs,
        scratch_shapes=scratch,
        input_output_aliases=aliases,
        compiler_params=params(),
        cost_estimate=pl.CostEstimate(
            flops=6 * 27 * chans * sum(sizes) * cells * 2 // COST_SHARE,
            bytes_accessed=4 * (chans + sum(sizes)) * cells // COST_SHARE,
            transcendentals=0,
        ),
        name="conv_" + mode,
    )(*args)


def grad_kernel(dims, others, *refs):
    padded, planes, height, width = dims
    xh, xl, cot, bit = refs[:4]
    done = refs[4 : 4 + others]
    *outs_refs, total = refs[4 + others :]
    outs = cot.shape[0]
    step = pl.program_id(0)
    span = 3 * padded
    half = 3 * span
    group = up_to(3 * outs, 128)

    @pl.when(step == 0)
    def _():
        total[...] = jnp.zeros_like(total)

    lane = lax.broadcasted_iota(jnp.int32, (outs, width), 1)
    first = lane == 0
    last = lane == width - 1
    lhs = []
    for src in (xh, xl):
        for i in range(3):
            window = src[step + i]
            lhs.append(
                jnp.concatenate(
                    [window[r * padded : r * padded + span] for r in range(height)], axis=1
                )
            )
    columns = []
    for block in range(height // ROWS):
        rows = jnp.swapaxes(cot[:, 0, pl.ds(ROWS * block, ROWS), :], 0, 1)
        for r in range(ROWS):
            c = rows[r]
            moved = [
                jnp.where(last, 0.0, pltpu.roll(c, width - 1, 1)),
                c,
                jnp.where(first, 0.0, pltpu.roll(c, 1, 1)),
            ]
            pieces = [split(m) for m in moved]
            gap = group - 3 * outs
            fill = [jnp.zeros((gap, width), BF16)] if gap else []
            columns.append(
                jnp.concatenate(
                    [p[0] for p in pieces] + fill + [p[1] for p in pieces] + fill, axis=0
                )
            )
    total[...] += lax.dot_general(
        jnp.concatenate(lhs, axis=0),
        jnp.concatenate(columns, axis=1),
        (((1,), (1,)), ((), ())),
        preferred_element_type=F32,
    )

    @pl.when(step == planes - 1)
    def _():
        summed = total[:half, :group] + total[:half, group:] + total[half:, :group]
        if len(outs_refs) == 1:
            outs_refs[0][...] = summed
        else:
            total[:half, :group] = summed
            rows = half // 2
            kept = pl.multiple_of(bit[0] * rows, 8)
            sent = pl.multiple_of((1 - bit[0]) * rows, 8)
            for ref, start in zip(outs_refs, (kept, sent)):
                for index, other in enumerate(done):
                    ref[index] = other[pl.ds(start, rows), :]
                ref[others] = total[pl.ds(start, rows), :group]


def kernel_grad(xh, xl, cot, bit, done=None):
    outs, planes, height, width = cot.shape
    padded = xh.shape[1] // (height + 2)
    group = up_to(3 * outs, 128)
    cells = planes * height * width
    rows = 9 * padded
    earlier = () if done is None else tuple(done)
    shape = (rows, group) if done is None else (len(earlier) + 1, rows // 2, group)
    shapes = [jax.ShapeDtypeStruct(shape, F32)] * (1 if done is None else 2)
    return pl.pallas_call(
        functools.partial(grad_kernel, (padded, planes, height, width), len(earlier)),
        grid=(planes,),
        in_specs=[WHOLE] * 2
        + [pl.BlockSpec((outs, 1, height, width), lambda d: (0, d, 0, 0)), SCALAR]
        + [WHOLE] * len(earlier),
        out_specs=[WHOLE] * len(shapes),
        out_shape=shapes,
        scratch_shapes=[pltpu.VMEM((2 * rows, 2 * group), F32)],
        compiler_params=params(),
        cost_estimate=pl.CostEstimate(
            flops=6 * 3 * rows * outs * cells * 2 // COST_SHARE,
            bytes_accessed=8 * outs * cells // COST_SHARE,
            transcendentals=0,
        ),
        name="kernel_grad",
    )(xh, xl, cot, bit, *earlier)


def three_parts(matrix, wide):
    hi, lo = split(matrix)
    parts = [hi, hi, lo]
    extra = wide - 3 * matrix.shape[1]
    if extra:
        parts.append(jnp.zeros((matrix.shape[0], extra), BF16))
    return jnp.concatenate(parts, axis=1)


def weight_kernel(groups, me, taps, forward, *refs):
    backward, turned = refs[:groups], refs[groups]
    cin, channels = taps.shape[1:]
    mine = channels // groups
    pad_in = up_to(cin, 16)
    pad_out = up_to(mine, 16)
    for k in range(3):
        blocks = []
        for tap in range(9):
            blocks.append(taps[3 * tap + k])
            if pad_in != cin:
                blocks.append(jnp.zeros((pad_in - cin, channels), F32))
        turned[...] = jnp.concatenate(blocks, axis=0).T
        for g in range(groups):
            owner = lax.rem(me[0] + g, groups)
            rows = turned[pl.ds(pl.multiple_of(owner * mine, mine), mine), :]
            forward[pl.ds(k * channels + g * mine, mine), :] = three_parts(
                rows, forward.shape[1]
            )
    for s in range(groups):
        owner = lax.rem(me[0] + s, groups)
        for k in range(3):
            blocks = []
            for tap in range(9):
                block = taps[26 - 3 * tap - k]
                chosen = block[:, :mine]
                for q in range(1, groups):
                    chosen = jnp.where(owner == q, block[:, q * mine : (q + 1) * mine], chosen)
                blocks.append(chosen)
                if pad_out != mine:
                    blocks.append(jnp.zeros((cin, pad_out - mine), F32))
            backward[s][pl.ds(k * cin, cin), :] = three_parts(
                jnp.concatenate(blocks, axis=1), backward[s].shape[1]
            )


def weight_matrices(me, taps, groups):
    _, cin, channels = taps.shape
    mine = channels // groups
    pad_in = up_to(cin, 16)
    wide_in = up_to(27 * pad_in, 128)
    wide_out = up_to(27 * up_to(mine, 16), 128)
    return pl.pallas_call(
        functools.partial(weight_kernel, groups),
        in_specs=[SCALAR, WHOLE],
        out_specs=[WHOLE] * (groups + 1),
        out_shape=[jax.ShapeDtypeStruct((3 * channels, wide_in), BF16)]
        + [jax.ShapeDtypeStruct((3 * cin, wide_out), BF16)] * groups,
        scratch_shapes=[pltpu.VMEM((channels, 9 * pad_in), F32)],
        compiler_params=params(0),
        name="weights",
    )(me, taps)


def finish_kernel(groups, scale, me, bit, mine_ref, other_ref, out):
    cin, channels = out.shape[1:]
    mine = channels // groups
    padded = 2 * mine_ref.shape[1] // 9
    low = bit[0] == 0
    totals = []
    for s in range(groups):
        a, b = mine_ref[s] * scale, other_ref[s] * scale
        totals.append(jnp.concatenate([jnp.where(low, a, b), jnp.where(low, b, a)], axis=0))
    for k in range(3):
        pieces = [t[:, k * mine : (k + 1) * mine] for t in totals]
        blocks = []
        for q in range(groups):
            source = lax.rem(q - me[0] + groups, groups)
            chosen = pieces[0]
            for s in range(1, groups):
                chosen = jnp.where(source == s, pieces[s], chosen)
            blocks.append(chosen)
        wide = jnp.concatenate(blocks, axis=1)
        for tap in range(9):
            out[3 * tap + k] = wide[tap * padded : tap * padded + cin]


def finish(me, bit, value, other, groups, cin, channels, scale):
    return pl.pallas_call(
        functools.partial(finish_kernel, groups, scale),
        in_specs=[SCALAR, SCALAR, WHOLE, WHOLE],
        out_specs=WHOLE,
        out_shape=jax.ShapeDtypeStruct((27, cin, channels), F32),
        compiler_params=params(0),
        name="finish",
    )(me, bit, value, other)


def add_kernel(count, *refs):
    total = refs[0][...]
    for ref in refs[1:count]:
        total = total + ref[...]
    refs[-1][...] = total


def add_pieces(own, pieces, whole, shape, first, block, plane_of):
    channels, out_planes, height, width = pieces[0].shape
    size = (block, 1, height, width)
    start = first // block
    here = pl.BlockSpec(size, lambda p, c: (c, p, 0, 0))
    args = [own, *pieces]
    specs = [pl.BlockSpec(size, lambda p, c: (start + c, p, 0, 0))] + [here] * len(pieces)
    aliases = {}
    if whole is not None:
        aliases[len(args)] = 0
        args.append(whole)
        specs.append(pl.BlockSpec(memory_space=pl.ANY))
    return pl.pallas_call(
        functools.partial(add_kernel, 1 + len(pieces)),
        grid=(out_planes, channels // block),
        in_specs=specs,
        out_specs=pl.BlockSpec(size, lambda p, c: (start + c, plane_of(p), 0, 0)),
        out_shape=jax.ShapeDtypeStruct(shape, F32),
        input_output_aliases=aliases,
        compiler_params=params(2),
        cost_estimate=pl.CostEstimate(
            flops=pieces[0].size, bytes_accessed=12 * pieces[0].size, transcendentals=0
        ),
        name="add_pieces",
    )(*args)


def cut_edges(field, bit):
    ends = field.shape[1] - 1
    to_sibling = lax.dynamic_slice_in_dim(field, (1 - bit[0]) * ends, 1, axis=1)
    to_neighbour = lax.dynamic_slice_in_dim(field, bit[0] * ends, 1, axis=1)
    return lax.optimization_barrier((field, to_sibling, to_neighbour))


def slab_halo(to_sibling, to_neighbour):
    count = lax.axis_size("slab")
    across = [(i, i + 1) for i in range(1, count - 1, 2)]
    across += [(j, i) for i, j in across]
    return slab_swap(to_sibling, 1), lax.ppermute(to_neighbour, "slab", across)


def slab_swap(value, bit):
    return lax.ppermute(
        value, "slab", [(i, i ^ bit) for i in range(lax.axis_size("slab"))]
    )


def per_device(activations, kernel, cotangent):
    groups = lax.axis_size("chan")
    slabs = lax.axis_size("slab")
    assert slabs > 1 and slabs & (slabs - 1) == 0 and groups > 1
    bits = [1 << b for b in range(1, slabs.bit_length() - 1)]
    me = lax.axis_index("chan").reshape(1)
    bit = lax.rem(lax.axis_index("slab"), 2).reshape(1)
    channels, taps, cin = kernel.shape
    mine = channels // groups
    planes, height, width = activations.shape[1:]

    quarter = max(mine // 4, 1)
    pieces = (mine - quarter, quarter)
    after = lax.optimization_barrier

    cots = [cotangent]
    for s in range(1, groups):
        cots.append(
            lax.ppermute(cotangent, "chan", [((i + s) % groups, i) for i in range(groups)])
        )
    activations, *edges = cut_edges(activations, bit)
    act_halo = slab_halo(*edges)
    forward, *backward = weight_matrices(me, kernel.transpose(1, 2, 0), groups)

    own_inner, *inner, xh, xl = conv(
        "inner", [activations], None, forward, bit, (mine,) * groups, 2, keep=True
    )
    own, xh, *act_halo = after((cotangent, xh, *act_halo))
    own, *edges = cut_edges(own, bit)
    *edges, xh = after((*edges, xh))
    cot_halo = slab_halo(*edges)
    own_outer, *outer, xh, xl = conv(
        "outer",
        [xh, xl],
        act_halo,
        forward,
        bit,
        (mine,) + pieces * (groups - 1),
        2,
        keep=True,
    )

    def next_swap(value):
        return slab_swap(value, bits.pop(0)) if bits else jnp.zeros_like(value)

    def to_owner(part, s):
        return lax.ppermute(part, "chan", [(i, (i + s) % groups) for i in range(groups)])

    got_inner = [to_owner(inner[s - 1], s) for s in range(1, groups)]
    got_outer = []
    for index in range(len(pieces)):
        parts = outer[index :: len(pieces)]
        got_outer.append([to_owner(parts[s - 1], s) for s in range(1, groups)])

    grads = list(kernel_grad(xh, xl, own, bit))
    (input_grad,) = conv("all", [own], cot_halo, backward[0], bit, (cin,), 4)
    for s in range(1, groups):
        cot, input_grad, *grads = after((cots[s], input_grad, *grads))
        cot, *edges = cut_edges(cot, bit)
        halo = slab_halo(*edges)
        if s < groups - 1:
            grads += kernel_grad(xh, xl, cot, bit)
        else:
            kept, sent = kernel_grad(xh, xl, cot, bit, grads)
            value = kept + slab_swap(sent, 1)
            value, cot = after((value, cot))
            other = next_swap(value)
        input_grad, ch, cl = conv(
            "inner", [cot], None, backward[s], bit, (cin,), 4, input_grad, keep=True
        )
        if s == groups - 1:
            other, ch, *halo = after((other, ch, *halo))
            value = value + other
            other = next_swap(value)
        (input_grad,) = conv(
            "outer", [ch, cl], halo, backward[s], bit, (cin,), 4, input_grad
        )

    other, input_grad = after((other, input_grad))
    value = value + other
    while len(bits) > 1:
        value = value + next_swap(value)
    *got_inner, value = after((*got_inner, value))
    other = next_swap(value)
    features = add_pieces(
        own_inner, got_inner, None, (mine, planes, height, width), 0,
        mine // 2, lambda p: p + 1,
    )
    other, features = after((other, features))
    value = value + other
    cells_all = planes * slabs * height * width
    weight_grad = finish(
        me, bit, value, slab_swap(value, 1), groups, cin, channels, 1.0 / math.sqrt(cells_all)
    )
    weight_grad, features = after((weight_grad, features))
    first = 0
    for got, size in zip(got_outer, pieces):
        *got, features = after((*got, features))
        features = add_pieces(
            own_outer, got, features, features.shape, first, size,
            lambda p: p * (planes - 1),
        )
        first += size
    return features, input_grad, weight_grad.transpose(2, 0, 1)


def solution(mesh):
    return jax.shard_map(
        per_device,
        mesh=mesh,
        in_specs=(
            P("chan", "slab", None, None),
            P(None, None, "chan"),
            P("chan", "slab", None, None),
        ),
        out_specs=(
            P("chan", "slab", None, None),
            P("chan", "slab", None, None),
            P(None, None, "chan"),
        ),
        check_vma=False,
    )
```
